256 devices in a mesh: tile: 64 (over z, x, core), mp: 4 (over y).
Axes of the slice: x: 4, y: 4, z: 8, core: 2. Of those that a mesh axis runs over, the one named last changes fastest.
Arguments:
- latent: bfloat16 [768, 384], P('tile'), may hold values from -19 to 19, as said below
- reward_grad: float32 [768, 384], P('tile'), may hold values from -6 to 6
- curvature: float32 [768, 384], P('tile'), may hold values from 0.3 to 3
- offsets: int32 [128, 2], P('tile'), may hold values from 0 to 736, as said below
- counts: int32 [768, 96], P('tile'), may hold values from 1 to 4, as said below
- w_in: bfloat16 [16, 640], replicated, may hold values from -3.2 to 3.2, as said below
- w_value: bfloat16 [640, 2560], P(None, 'mp'), may hold values from -0.25 to 0.25
- w_gate: bfloat16 [640, 2560], P(None, 'mp'), may hold values from -0.25 to 0.25
- w_down: bfloat16 [2560, 640], P('mp'), may hold values from -0.125 to 0.125
- w_out: bfloat16 [640, 16], replicated, may hold values from -0.25 to 0.25
Outputs:
- blended: float32 [768, 384], P('tile')
- grad_in: float32 [16, 640], replicated
- grad_value: float32 [640, 2560], P(None, 'mp')
- grad_gate: float32 [640, 2560], P(None, 'mp')
- grad_down: float32 [2560, 640], P('mp')
- grad_out: float32 [640, 16], replicated
The draws below stay inside these ranges and needn't reach their ends.
Inputs may be any that keep to these rules, and one draw needn't show every extreme that they name: `offsets`: the corners are the points of a grid of 32 by 4 points spaced 24, each point taken by exactly one tile in a random order, each moved by at most 4 along each direction; the grid's first row and column stay at 0 and its last row and column are clamped to 736 and 64. The tiles cover every cell of the canvas. `counts`: the number of tiles whose 32 x 32 square holds the cell. `latent`: Real-valued. `w_in`: Real-valued.
All inputs are finite; a program needn't handle non-finite values.
Results may differ from the reference program's by a relative error of at most 0.003.
The reference program's roundings to bfloat16 on the way count: a program that leaves them out, or rounds other values in their place, can miss the bound.
Values may be sent and summed in bfloat16 or wider, within the bound.
A program may use at most 64 MiB of HBM per device.

```python
import math
import jax
import jax.numpy as jnp
from jax import lax

C = 4
D = 640
FF = 2560
S = 32
SPACING = 24
JITTER = 4
F = 16
TT = 256
H = 768
W = 96
TILES = 128


def grid_corners(key):
    base_key = jax.random.fold_in(key, 11)
    row_key, col_key, order_key = jax.random.split(base_key, 3)
    grid_cols = W // SPACING
    row_jitter = jax.random.randint(row_key, (TILES,), -JITTER, JITTER + 1)
    col_jitter = jax.random.randint(col_key, (TILES,), -JITTER, JITTER + 1)
    grid_cells = jax.random.permutation(order_key, TILES)
    grid_row = grid_cells // grid_cols
    grid_col = grid_cells % grid_cols
    row_start = jnp.where(grid_row == 0, 0, jnp.clip(grid_row * SPACING + row_jitter, 0, H - S))
    col_start = jnp.where(grid_col == 0, 0, jnp.clip(grid_col * SPACING + col_jitter, 0, W - S))
    return jnp.stack([row_start, col_start], axis=1).astype(jnp.int32)


def draw_offsets(key, part):
    return grid_corners(key)


def draw_counts(key, part):
    corners = grid_corners(key)
    row_ids = jnp.arange(H, dtype=jnp.int32)
    col_ids = jnp.arange(W, dtype=jnp.int32)
    row_cover = ((row_ids[None, :] >= corners[:, 0:1]) & (row_ids[None, :] < corners[:, 0:1] + S)).astype(jnp.int32)
    col_cover = ((col_ids[None, :] >= corners[:, 1:2]) & (col_ids[None, :] < corners[:, 1:2] + S)).astype(jnp.int32)
    return jnp.sum(row_cover[:, :, None] * col_cover[:, None, :], axis=0).astype(jnp.int32)


def draw_latent(key, part):
    base_key, spread_key = jax.random.split(jax.random.fold_in(key, 23))
    spread = jnp.exp(jax.random.uniform(spread_key, (H, W * C), minval=-1.15, maxval=1.15))
    values = jnp.clip(jax.random.normal(base_key, (H, W * C)), -6.0, 6.0)
    return (values * spread).astype(jnp.float32).astype(jnp.bfloat16)


def draw_w_in(key, part):
    base_key, column_key = jax.random.split(jax.random.fold_in(key, 37), 2)
    column_scale = jnp.exp(jax.random.uniform(column_key, (1, D), minval=-1.15, maxval=1.15))
    values = jnp.clip(jax.random.normal(base_key, (F, D)), -4.0, 4.0)
    return (values * column_scale * F ** (-0.5)).astype(jnp.float32).astype(jnp.bfloat16)


def steps_of(own_key, dims, pieces, least, top_value):
    def one(axis_at, blocks):
        heights = jax.random.uniform(jax.random.fold_in(jax.random.fold_in(own_key, 6), axis_at), (blocks,), jnp.float32, least / len(pieces), top_value / len(pieces))
        return jnp.repeat(jnp.exp(heights), dims[axis_at] // blocks).reshape((-1,) + (1,) * (len(dims) - axis_at - 1))

    factor_of = one(*pieces[0])
    for cut in pieces[1:]:
        factor_of = factor_of * one(*cut)
    return factor_of


def bell_draw(stream_key, shape, width, bound, pieces=(), kind=jnp.bfloat16):
    result = jax.random.normal(stream_key, shape, jnp.float32) * width
    if len(pieces) > 0:
        result = steps_of(stream_key, shape, pieces, -0.22, 0.18) * result
    return jnp.clip(result, min=-bound, max=bound).astype(kind)


def setup_inputs(seed: int = 0) -> dict:
    splits = jax.random.split(jax.random.key(seed), 11)
    latent = draw_latent(jax.random.fold_in(splits[10], 71), 0)
    reward_grad = bell_draw(splits[1], (H, W * C), 1.0, 6.0, ((0, 64),), jnp.float32)
    curvature = jnp.clip(jnp.exp(math.log(3.0) - 2.3025851 * jax.random.uniform(splits[2], (H, W * C), jnp.float32) ** steps_of(splits[2], (H, W * C), ((0, 64),), -0.2, 0.2)), 0.3, 3.0)
    offsets = draw_offsets(jax.random.fold_in(splits[10], 71), 0)
    counts = draw_counts(jax.random.fold_in(splits[10], 71), 0)
    w_in = draw_w_in(jax.random.fold_in(splits[10], 71), 0)
    w_value = bell_draw(splits[6], (D, FF), D ** -0.5, 0.25, ((1, 4),))
    w_gate = bell_draw(splits[7], (D, FF), D ** -0.5, 0.25, ((1, 4),))
    w_down = bell_draw(splits[8], (FF, D), FF ** -0.5, 0.125, ((0, 4),))
    w_out = bell_draw(splits[9], (D, F), D ** -0.5, 0.25)
    return dict(latent=latent, reward_grad=reward_grad, curvature=curvature, offsets=offsets, counts=counts, w_in=w_in, w_value=w_value, w_gate=w_gate, w_down=w_down, w_out=w_out)


layer_eps = 1e-05
root_half = 0.7071067811865476
inv_root_two_pi = 0.3989422804014327

def product(left, right):
    return jnp.dot(left.astype(jnp.float32), right.astype(jnp.float32), preferred_element_type=jnp.float32)

def gelu_value(inputs):
    return 0.5 * inputs * (1.0 + lax.erf(inputs * root_half))

def gelu_slope(inputs):
    return 0.5 * (1.0 + lax.erf(inputs * root_half)) + inputs * jnp.exp(-0.5 * inputs * inputs) * inv_root_two_pi

def patchify(cropped, channels):
    half_side = cropped.shape[0] // 2
    return cropped.reshape(half_side, 2, half_side, 2 * channels).transpose(0, 2, 1, 3).reshape(half_side * half_side, 4 * channels)

def unpatch(tokens, tile_side, channels):
    half_side = tile_side // 2
    token_rows = tokens.shape[0] // half_side
    return tokens.reshape(token_rows, half_side, 2, 2 * channels).transpose(0, 2, 1, 3).reshape(2 * token_rows, tile_side * channels)

def layer_norm(hidden):
    values = hidden.astype(jnp.float32)
    center = values - lax.optimization_barrier(jnp.mean(values, axis=-1, keepdims=True))
    variance = lax.optimization_barrier(jnp.mean(center * center, axis=-1, keepdims=True))
    inv_scale = lax.rsqrt(variance + layer_eps)
    return (center * inv_scale, inv_scale)

def norm_backward(normed, inv_scale, d_unit):
    centered = d_unit - lax.optimization_barrier(jnp.mean(d_unit, axis=-1, keepdims=True))
    return inv_scale * (centered - normed * lax.optimization_barrier(jnp.mean(d_unit * normed, axis=-1, keepdims=True)))

def forward_tile(patches, weights):
    w_in, w_value, w_gate, w_down, w_out = weights
    hidden = product(patches, w_in).astype(jnp.bfloat16)
    normed, inv_scale = layer_norm(hidden)
    unit_in = normed.astype(jnp.bfloat16)
    value_proj = product(unit_in, w_value)
    gate_proj = product(unit_in, w_gate)
    active = (value_proj * gelu_value(gate_proj)).astype(jnp.bfloat16)
    ff_out = product(active, w_down)
    noise_pred = product(hidden, w_out) + jnp.dot(ff_out, w_out.astype(jnp.float32), precision=lax.Precision.HIGHEST)
    return (noise_pred, (hidden, normed, inv_scale, unit_in, value_proj, gate_proj, active, ff_out))

def backward_tile(patches, cot_tokens, saved, weights):
    w_in, w_value, w_gate, w_down, w_out = weights
    hidden, normed, inv_scale, unit_in, value_proj, gate_proj, active, ff_out = saved
    d_feat = product(cot_tokens, jnp.transpose(w_out))
    d_feat_b = d_feat.astype(jnp.bfloat16)
    d_active = product(d_feat_b, jnp.transpose(w_down))
    d_value = (d_active * gelu_value(gate_proj)).astype(jnp.bfloat16)
    d_gate = (d_active * value_proj * gelu_slope(gate_proj)).astype(jnp.bfloat16)
    d_unit = product(d_value, jnp.transpose(w_value)) + product(d_gate, jnp.transpose(w_gate))
    d_hidden = (d_feat + norm_backward(normed, inv_scale, d_unit)).astype(jnp.bfloat16)
    grad_in = product(jnp.transpose(patches), d_hidden)
    grad_value = product(jnp.transpose(unit_in), d_value)
    grad_gate = product(jnp.transpose(unit_in), d_gate)
    grad_down = product(jnp.transpose(active), d_feat_b)
    grad_out = product(jnp.transpose(hidden), cot_tokens) + jnp.dot(jnp.transpose(ff_out), cot_tokens.astype(jnp.float32), precision=lax.Precision.HIGHEST)
    return (grad_in, grad_value, grad_gate, grad_down, grad_out)

def reference(latent, reward_grad, curvature, offsets, counts, w_in, w_value, w_gate, w_down, w_out):
    weights = (w_in, w_value, w_gate, w_down, w_out)

    def crop_at(canvas, corner):
        return lax.dynamic_slice(canvas, (corner[0], corner[1] * C), (S, S * C))

    def predict(corner):
        patches = patchify(crop_at(latent, corner), C)
        noise_pred, saved = forward_tile(patches, weights)
        return unpatch(noise_pred, S, C)
    tile_noise = lax.map(predict, offsets)

    def place(canvas, item):
        corner, piece = item
        start = (corner[0], corner[1] * C)
        current = lax.dynamic_slice(canvas, start, (S, S * C))
        return (lax.dynamic_update_slice(canvas, current + piece, start), None)
    blend_total, unused = lax.scan(place, jnp.zeros((H, W * C), jnp.float32), (offsets, tile_noise))
    cover_count = jnp.repeat(counts, C, axis=1).astype(jnp.float32)
    blended = blend_total / cover_count
    scale_factor = 16.0 / math.sqrt(TILES * TT)
    cotangent = ((reward_grad - curvature * blended) / cover_count * scale_factor).astype(jnp.bfloat16)

    def accumulate(carry, corner):
        patches = patchify(crop_at(latent, corner), C)
        noise_pred, saved = forward_tile(patches, weights)
        cot_tokens = patchify(crop_at(cotangent, corner), C)
        terms = backward_tile(patches, cot_tokens, saved, weights)
        return (tuple((first + second for first, second in zip(carry, terms))), None)
    initial = (jnp.zeros((F, D), jnp.float32), jnp.zeros((D, FF), jnp.float32), jnp.zeros((D, FF), jnp.float32), jnp.zeros((FF, D), jnp.float32), jnp.zeros((D, F), jnp.float32))
    totals, unused_two = lax.scan(accumulate, initial, offsets)
    grad_in, grad_value, grad_gate, grad_down, grad_out = totals
    return (blended, grad_in, grad_value, grad_gate, grad_down, grad_out)
```

```python
import functools
import math

import jax
import jax.numpy as jnp
from jax import lax
from jax.experimental import pallas as pl
from jax.experimental.pallas import tpu as pltpu
from jax.sharding import PartitionSpec as P

MESH = pl.DeviceIdType.MESH
bf16 = jnp.bfloat16
f32 = jnp.float32

SIDE = 32
HALF = 16
SPACING = 24
JITTER = 4
CH = 4
F = 16
D = 640
COLS = 384
CELLS = 96
SLAB = 12
REGION = 48
GRID_ROWS = 32
MP = 4
TILES = 128
layer_eps = 1e-05
root_half = 0.7071067811865476
inv_root_two_pi = 0.3989422804014327
SCALE = 16.0 / math.sqrt(TILES * HALF * HALF)
PAY = 2048


def dot(left, right, dims=((1,), (0,))):
    return lax.dot_general(left, right, (dims, ((), ())), preferred_element_type=f32)


NT = ((1,), (1,))
TN = ((0,), (0,))


def iota(shape, dim):
    return lax.broadcasted_iota(jnp.int32, shape, dim)


def one_hot(cond):
    return jnp.where(cond, 1.0, 0.0).astype(bf16)


def split3(x):
    hi = x.astype(bf16)
    rest = x - hi.astype(f32)
    mid = rest.astype(bf16)
    lo = (rest - mid.astype(f32)).astype(bf16)
    return hi, mid, lo


def split2(x):
    hi = x.astype(bf16)
    return hi, (x - hi.astype(f32)).astype(bf16)


def feature_of(lane):
    return (lane // 128) * 8 + lane % 8


def main_kernel(
    lat_h, rew_h, cur_h, cnt_h, win_h, wv_h, wg_h, wd_h, wo_h,
    blend_o, g_o, pin_o, pout_o,
    lat_s, cnt_s, rew_v, cur_v, win_v, wv, wg, wd, wo_v,
    regf, cntf, x_s, unit_s, hid_s, gel_s, vs_s, val_s, gate_s, act_s,
    part_s, rs_send, rs_in, cot_in, blend_in, cot_mine, blend_mine, wdo_s, woe_s,
    pay_s, pay_send, pay_in, z_in, z_mine, g_in, st_s, st_o, y_in, y_mine, p_in,
    loc_sem, send_sem, halo_sem, rs_sem, cot_sem, blend_sem, pay_sem, z_sem, g_sem, y_sem, p_sem,
):
    t = lax.axis_index("tile")
    p = lax.axis_index("mp")
    chip = t // 2
    k = t % 2
    up_chip = (chip + GRID_ROWS - 1) % GRID_ROWS
    down_chip = (chip + 1) % GRID_ROWS
    beside = jnp.where(k == 0, up_chip, down_chip)
    base8 = (t // 8) * 8
    member = t % 8
    plane = t // 8

    loads = []
    for n, (src, dst) in enumerate([
        (lat_h, lat_s.at[1 + k]), (cnt_h, cnt_s.at[1 + k]), (wd_h, wd), (wo_h, wo_v), (win_h, win_v),
        (wv_h, wv), (wg_h, wg), (rew_h, rew_v), (cur_h, cur_v),
    ]):
        copy = pltpu.make_async_copy(src, dst, loc_sem.at[n])
        copy.start()
        loads.append(copy)

    own_chip = [((2 * chip + (k + dk) % 2), (p + dq) % MP, (k + dk) % 2) for dk in range(2) for dq in range(MP)][1:]
    group = [(base8 + (member + n) % 8, (member + n) % 8) for n in range(1, 8)]
    planes = [(((plane + n) % 8) * 8 + member, (plane + n) % 8) for n in range(1, 8)]

    barrier = pltpu.get_barrier_semaphore()
    hellos = [(a, b) for a, b, _ in own_chip]
    hellos += [(2 * c + kk, q) for c in (up_chip, down_chip) for kk in range(2) for q in range(MP)]
    hellos += [(a, p) for a, _ in group] + [(a, p) for a, _ in planes]
    for target in hellos:
        pl.semaphore_signal(barrier, inc=1, device_id=target, device_id_type=MESH)
    pl.semaphore_wait(barrier, len(hellos))

    sent = []

    def send(src, dst, sem, target):
        copy = pltpu.make_async_remote_copy(
            src_ref=src, dst_ref=dst, send_sem=send_sem.at[len(sent)], recv_sem=sem,
            device_id=target, device_id_type=MESH,
        )
        copy.start()
        sent.append(copy)

    def arrive(dst, sem):
        pltpu.make_async_remote_copy(
            src_ref=dst, dst_ref=dst, send_sem=send_sem.at[0], recv_sem=sem,
            device_id=(t, p), device_id_type=MESH,
        ).wait_recv()

    far_slot = 3 * (1 - k)
    for target, slot in [((2 * chip + 1 - k, p), 1 + k), ((2 * beside, p), far_slot), ((2 * beside + 1, p), far_slot)]:
        send(lat_h, lat_s.at[slot], halo_sem.at[0, slot], target)
        send(cnt_h, cnt_s.at[slot], halo_sem.at[1, slot], target)

    lane256 = iota((1, 256), 1)
    expand = one_hot(iota((F, 256), 0) == feature_of(iota((F, 256), 1)))
    tj_mask = (iota((HALF, 1, 256), 2) % 128) // 8 == iota((HALF, 1, 256), 0)

    for copy in loads[2:5]:
        copy.wait()
    woe = dot(wo_v[...], expand).astype(bf16)
    woe_s[...] = woe
    wdo = dot(wd[...], woe)
    wdo_hi, wdo_lo = split2(wdo)
    wdo_s[0] = wdo_hi
    wdo_s[1] = wdo_lo
    win = win_v[...]
    wrep = dot(expand, win, TN).astype(bf16)

    loads[0].wait()
    loads[1].wait()
    for slot in (2 - k, 0, 3):
        arrive(lat_s.at[slot], halo_sem.at[0, slot])
        arrive(cnt_s.at[slot], halo_sem.at[1, slot])

    for slot in range(4):
        regf[SLAB * slot : SLAB * slot + SLAB, :] = lat_s[slot].astype(f32)
        cntf[SLAB * slot : SLAB * slot + SLAB, :] = cnt_s[slot].astype(f32)

    lane96 = iota((8, CELLS), 1)
    row_win = jnp.where(cntf[8:16, :] == 2.0, 1.0, 0.0)
    col_win = jnp.where(cntf[24:32, :] == 2.0, 1.0, 0.0)
    first_row = iota((8, CELLS), 0) == 0
    selects = []
    for j in range(2):
        c = 2 * k + j
        n_row = jnp.sum(jnp.where(lane96 == SPACING * c + 12, row_win, 0.0), axis=1, keepdims=True)
        n_row = jnp.sum(n_row, axis=0, keepdims=True)
        row = 16.0 - n_row
        row = jnp.where(chip == 0, 12.0, jnp.where(chip == GRID_ROWS - 1, 4.0, row))
        near = first_row & (lane96 >= SPACING * c - JITTER) & (lane96 < SPACING * c + JITTER)
        n_col = jnp.sum(jnp.where(near, col_win, 0.0), axis=1, keepdims=True)
        n_col = jnp.sum(n_col, axis=0, keepdims=True)
        col = (SPACING * c + JITTER).astype(f32) - n_col
        col = jnp.where(c == 0, 0.0, jnp.where(c == 3, float(CELLS - SIDE), col))
        m = iota((SIDE, REGION), 0)
        pick = (2 * (m % HALF) + m // HALF).astype(f32) + row
        sel_r = one_hot(iota((SIDE, REGION), 1).astype(f32) == pick)
        sel_c = one_hot(iota((COLS, 128), 0).astype(f32) == iota((COLS, 128), 1).astype(f32) + CH * col)
        m = iota((REGION, 3 * SIDE), 1) % SIDE
        pick = (2 * (m % HALF) + m // HALF).astype(f32) + row
        put_r = one_hot(iota((REGION, 3 * SIDE), 0).astype(f32) == pick)
        selects.append((sel_r, sel_c, put_r))

    def patches_of(region):
        tiles = []
        for sel_r, sel_c, _ in selects:
            rows = dot(sel_r, region).astype(bf16)
            crop = dot(rows, sel_c)
            pair = jnp.concatenate([crop[:HALF], crop[HALF:]], axis=1)
            full = jnp.where(tj_mask, pair.reshape(1, HALF, 256), 0.0)
            tiles.append(full.reshape(HALF * HALF, 256))
        return jnp.concatenate(tiles, axis=0)

    xf = patches_of(regf[...].astype(bf16))
    x = xf.astype(bf16)
    x_s[...] = x
    hidden = dot(x, wrep).astype(bf16)
    hid_s[...] = hidden
    values = hidden.astype(f32)
    center = values - jnp.mean(values, axis=-1, keepdims=True)
    variance = jnp.mean(center * center, axis=-1, keepdims=True)
    inv = lax.rsqrt(variance + layer_eps)
    unit = (center * inv).astype(bf16)
    unit_s[...] = unit

    loads[5].wait()
    loads[6].wait()
    value = dot(unit, wv[...])
    gate = dot(unit, wg[...])
    phi = 0.5 * (1.0 + lax.erf(gate * root_half))
    gel = gate * phi
    act = (value * gel).astype(bf16)
    act_s[...] = act
    gel_s[...] = gel
    val_s[...] = value
    gate_s[...] = gate
    vs_s[...] = value * (phi + gate * jnp.exp(-0.5 * gate * gate) * inv_root_two_pi)

    noise = dot(act, wdo_s[0]) + dot(act, wdo_s[1])
    own = dot(hid_s[...], woe_s[...])
    noise = noise + jnp.where(p == 0, own, 0.0)
    placed = None
    for j in range(2):
        block = noise[256 * j : 256 * j + 256].reshape(HALF, HALF, 256)
        crop = jnp.sum(jnp.where(tj_mask, block, 0.0), axis=0)
        stack = jnp.concatenate(
            [part[:, 128 * a : 128 * a + 128] for part in split3(crop) for a in range(2)], axis=0
        )
        wide = dot(stack, selects[j][1], NT).astype(bf16)
        term = dot(selects[j][2], wide)
        placed = term if placed is None else placed + term
    part_s[...] = placed
    for g in range(16):
        rs_send[g] = part_s[3 * g : 3 * g + 3, :]

    for dev, q, kk in own_chip:
        send(rs_send.at[4 + 4 * kk + q], rs_in.at[4 * k + p], rs_sem.at[4 * k + p], (dev, q))
    for q in range(MP):
        send(rs_send.at[q], rs_in.at[8 + 4 * k + p], rs_sem.at[8 + 4 * k + p], (2 * up_chip + 1, q))
        send(rs_send.at[12 + q], rs_in.at[8 + 4 * k + p], rs_sem.at[8 + 4 * k + p], (2 * down_chip, q))
    rs_in[4 * k + p] = rs_send[4 + 4 * k + p]

    xi = xf * inv
    xi_hi, xi_lo = split2(xi)
    pt = dot(expand, x, NT).astype(bf16)
    pit = jnp.concatenate([dot(expand, xi_hi, NT).astype(bf16), dot(expand, xi_lo, NT).astype(bf16)], axis=0)
    for copy in loads[7:9]:
        copy.wait()
    spread = one_hot(iota((CELLS, COLS), 0) == iota((CELLS, COLS), 1) // CH)
    cover = dot(cnt_s[1 + k].astype(f32).astype(bf16), spread)
    rew = rew_v[...]
    cur = cur_v[...]

    def my_rows(slab):
        out = slab[0:3]
        for q in range(1, MP):
            out = jnp.where(p == q, slab[3 * q : 3 * q + 3], out)
        return out

    cover3 = my_rows(cover)
    rew3 = my_rows(rew)
    cur3 = my_rows(cur)

    for dev, q, kk in own_chip:
        arrive(rs_in.at[4 * kk + q], rs_sem.at[4 * kk + q])
    for slot in range(8, 16):
        arrive(rs_in.at[slot], rs_sem.at[slot])
    total = rs_in[0]
    for slot in range(1, 16):
        total = total + rs_in[slot]
    blend3 = total / cover3
    cot3 = ((rew3 - cur3 * blend3) / cover3 * SCALE).astype(bf16).astype(f32)
    blend_mine[...] = blend3
    cot_mine[...] = cot3
    for dev, q, kk in own_chip:
        send(cot_mine, cot_in.at[4 + 4 * k + p], cot_sem.at[4 + 4 * k + p], (dev, q))
    slot = 12 * (1 - k) + p
    for kk in range(2):
        for q in range(MP):
            send(cot_mine, cot_in.at[slot], cot_sem.at[slot], (2 * beside + kk, q))
    for dq in range(1, MP):
        send(blend_mine, blend_in.at[p], blend_sem.at[p], (t, (p + dq) % MP))
    cot_in[4 + 4 * k + p] = cot3
    blend_in[p] = blend3

    for dev, q, kk in own_chip:
        arrive(cot_in.at[4 + 4 * kk + q], cot_sem.at[4 + 4 * kk + q])
    for q in range(MP):
        arrive(cot_in.at[q], cot_sem.at[q])
        arrive(cot_in.at[12 + q], cot_sem.at[12 + q])
    for g in range(16):
        regf[3 * g : 3 * g + 3, :] = cot_in[g]

    y = patches_of(regf[...].astype(bf16)).astype(bf16)
    dfb = dot(y, woe_s[...], NT).astype(bf16)
    d_act = dot(dfb, wd[...], NT)
    dv = (d_act * gel_s[...]).astype(bf16)
    dg = (d_act * vs_s[...]).astype(bf16)
    m2 = jnp.sum(dv.astype(f32) * val_s[...] + dg.astype(f32) * gate_s[...], axis=1, keepdims=True) * (1.0 / D)
    ct = dot(expand, y, NT).astype(bf16)
    gv = dot(pit, dv)
    gg = dot(pit, dg)
    gd = dot(ct, act_s[...])
    xm_hi, xm_lo = split2(xi * m2)
    b_w = dot(pit, xm_hi) + dot(pit, xm_lo)
    b_w = b_w[:F] + b_w[F:]
    a_w = dot(pt, y)
    at_w = dot(ct, x_s[...])

    def fold(wide):
        halves = []
        for a in range(2):
            part = wide[:, 128 * a : 128 * a + 128]
            for shift in (64, 32, 16, 8):
                part = part + pltpu.roll(part, shift, 1)
            halves.append(part)
        return halves

    lane128 = iota((F, 128), 1)
    small = jnp.zeros((F, 128), f32)
    for n, half in enumerate(fold(a_w) + fold(b_w) + fold(at_w)):
        small = jnp.where(lane128 // 8 == n, half, small)
    pay_s[:, 0:D] = gv[:F] + gv[F:]
    pay_s[:, D : 2 * D] = gg[:F] + gg[F:]
    pay_s[:, 2 * D : 3 * D] = gd
    pay_s[:, 3 * D : PAY] = small
    for c in range(8):
        pay_send[c] = pay_s[2 * c : 2 * c + 2, :]

    for dev, c in group:
        send(pay_send.at[c], pay_in.at[member], pay_sem.at[member], (dev, p))
    pay_in[member] = pay_send[member]
    for dev, c in group:
        arrive(pay_in.at[c], pay_sem.at[c])
    rows = pay_in[0]
    for c in range(1, 8):
        rows = rows + pay_in[c]
    z_mine[...] = rows
    for dev, c in planes:
        send(z_mine, z_in.at[plane], z_sem.at[plane], (dev, p))
    z_in[plane] = rows
    for dev, c in planes:
        arrive(z_in.at[c], z_sem.at[c])
    rows = z_in[0]
    for c in range(1, 8):
        rows = rows + z_in[c]
    g_in[member] = rows
    for dev, c in group:
        send(g_in.at[member], g_in.at[member], g_sem.at[member], (dev, p))

    def rows_dot(piece, right, dims):
        hi, mid, lo = split3(piece)
        width = piece.shape[1]
        st_s[0:2, 0:width] = hi.astype(f32)
        st_s[2:4, 0:width] = mid.astype(f32)
        st_s[4:6, 0:width] = lo.astype(f32)
        st_o[...] = dot(st_s[:, 0:width].astype(bf16), right, dims)
        return st_o[0:2, :] + st_o[2:4, :] + st_o[4:6, :]

    st_s[...] = jnp.zeros_like(st_s)
    small = rows[:, 3 * D : PAY]
    r16 = iota((128, F), 0)
    f16 = iota((128, F), 1)
    from_b = dot(one_hot(r16 == f16 + F), win).astype(bf16)
    from_t = dot(one_hot(r16 == f16 + 2 * F), win).astype(bf16)
    from_a = dot(one_hot(r16 == f16), wo_v[...], NT).astype(bf16)
    inner = rows_dot(rows[:, 0:D], wv[...], NT) + rows_dot(rows[:, D : 2 * D], wg[...], NT)
    inner = inner - rows_dot(small, from_b, ((1,), (0,)))
    inner = inner - jnp.mean(inner, axis=1, keepdims=True)
    y_mine[:, 0:D] = inner + 0.25 * rows_dot(small, from_a, ((1,), (0,)))
    outer = rows_dot(rows[:, 2 * D : 3 * D], wd[...], ((1,), (0,)))
    y_mine[:, D : 2 * D] = outer + 0.25 * rows_dot(small, from_t, ((1,), (0,)))
    y_in[p] = y_mine[...]
    for dq in range(1, MP):
        send(y_mine, y_in.at[p], y_sem.at[p], (t, (p + dq) % MP))
    for dq in range(1, MP):
        q = (p + dq) % MP
        arrive(y_in.at[q], y_sem.at[q])
    p_in[member] = y_in[0] + y_in[1] + y_in[2] + y_in[3]
    for dev, c in group:
        send(p_in.at[member], p_in.at[member], p_sem.at[member], (dev, p))

    for dq in range(1, MP):
        q = (p + dq) % MP
        arrive(blend_in.at[q], blend_sem.at[q])
    for q in range(MP):
        blend_o[3 * q : 3 * q + 3, :] = blend_in[q]
    for dev, c in group:
        arrive(g_in.at[c], g_sem.at[c])
    for c in range(8):
        g_o[2 * c : 2 * c + 2, :] = g_in[c][:, 0 : 3 * D]
    for dev, c in group:
        arrive(p_in.at[c], p_sem.at[c])
    for c in range(8):
        pin_o[2 * c : 2 * c + 2, :] = p_in[c][:, 0:D]
        pout_o[2 * c : 2 * c + 2, :] = p_in[c][:, D : 2 * D]
    for copy in sent:
        copy.wait_send()


def final_kernel(blend, g, pin, pout, win, wo, blend_o, gin_o, gv_o, gg_o, gd_o, gout_o):
    blend_o[...] = blend[...]
    gin_o[...] = pin[...]
    gout_o[...] = jnp.transpose(pout[...])
    w = win[...]
    w3 = jnp.concatenate([w, w, w], axis=0)
    mean = jnp.mean(w.astype(f32), axis=1, keepdims=True)
    eye = one_hot(iota((F, F), 0) == iota((F, F), 1))
    wot = dot(eye, wo[...], NT).astype(bf16)
    wot3 = jnp.concatenate([wot, wot, wot], axis=0)
    for n, out in enumerate((gv_o, gg_o)):
        rows = g[:, D * n : D * n + D]
        stack = jnp.concatenate(split3(rows), axis=0)
        out[...] = dot(w3, stack, TN) - jnp.sum(mean * rows, axis=0, keepdims=True)
    stack = jnp.concatenate(split3(g[:, 2 * D : 3 * D]), axis=0)
    gd_o[...] = dot(stack, wot3, TN)


def per_device(latent, reward_grad, curvature, offsets, counts, w_in, w_value, w_gate, w_down, w_out):
    vm = pltpu.VMEM
    any_spec = pl.BlockSpec(memory_space=pl.ANY)
    vm_spec = pl.BlockSpec(memory_space=pltpu.VMEM)
    tokens = 2 * HALF * HALF
    dma = pltpu.SemaphoreType.DMA
    scratch = [
        vm((4, SLAB, COLS), bf16), vm((4, SLAB, CELLS), jnp.int32), vm((SLAB, COLS), f32), vm((SLAB, COLS), f32),
        vm((F, D), bf16), vm((D, D), bf16), vm((D, D), bf16), vm((D, D), bf16), vm((D, F), bf16),
        vm((REGION, COLS), f32), vm((REGION, CELLS), f32), vm((tokens, 256), bf16), vm((tokens, D), bf16),
        vm((tokens, D), bf16), vm((tokens, D), f32), vm((tokens, D), f32), vm((tokens, D), f32), vm((tokens, D), f32),
        vm((tokens, D), bf16),
        vm((REGION, COLS), f32), vm((16, 3, COLS), f32), vm((16, 3, COLS), f32), vm((16, 3, COLS), f32),
        vm((MP, 3, COLS), f32), vm((3, COLS), f32), vm((3, COLS), f32), vm((2, D, 256), bf16), vm((D, 256), bf16),
        vm((F, PAY), f32), vm((8, 2, PAY), f32), vm((8, 2, PAY), f32), vm((8, 2, PAY), f32), vm((2, PAY), f32),
        vm((8, 2, PAY), f32), vm((8, D), f32), vm((8, D), f32), vm((MP, 2, 2 * D), f32), vm((2, 2 * D), f32),
        vm((8, 2, 2 * D), f32),
        dma((9,)), dma((70,)), dma((2, 4)), dma((16,)), dma((16,)), dma((MP,)), dma((8,)), dma((8,)), dma((8,)),
        dma((MP,)), dma((8,)),
    ]
    sds = jax.ShapeDtypeStruct
    blend, g, pin, pout = pl.pallas_call(
        main_kernel,
        out_shape=(sds((SLAB, COLS), f32), sds((F, 3 * D), f32), sds((F, D), f32), sds((F, D), f32)),
        in_specs=[any_spec] * 9,
        out_specs=(vm_spec,) * 4,
        scratch_shapes=scratch,
        compiler_params=pltpu.CompilerParams(
            collective_id=0, has_side_effects=True, vmem_limit_bytes=56 * 1024 * 1024
        ),
        name="tile_gradients",
    )(latent, reward_grad, curvature, counts, w_in, w_value, w_gate, w_down, w_out)
    return pl.pallas_call(
        final_kernel,
        out_shape=(
            sds((SLAB, COLS), f32), sds((F, D), f32), sds((D, D), f32), sds((D, D), f32), sds((D, D), f32),
            sds((D, F), f32),
        ),
        in_specs=[vm_spec] * 6,
        out_specs=(vm_spec,) * 6,
        name="weight_outputs",
    )(blend, g, pin, pout, w_in, w_out)


def solution(mesh):
    return jax.shard_map(
        per_device,
        mesh=mesh,
        in_specs=(
            P("tile", None), P("tile", None), P("tile", None), P("tile", None), P("tile", None), P(),
            P(None, "mp"), P(None, "mp"), P("mp", None), P(),
        ),
        out_specs=(P("tile", None), P(), P(None, "mp"), P(None, "mp"), P("mp", None), P()),
        check_vma=False,
    )
```

```python
import functools
import math

import jax
import jax.numpy as jnp
from jax import lax
from jax.experimental import pallas as pl
from jax.experimental.pallas import tpu as pltpu
from jax.sharding import PartitionSpec as P

MESH = pl.DeviceIdType.MESH
bf16 = jnp.bfloat16
f32 = jnp.float32

SIDE = 32
HALF = 16
SPACING = 24
JITTER = 4
CH = 4
F = 16
D = 640
COLS = 384
CELLS = 96
SLAB = 12
REGION = 48
GRID_ROWS = 32
MP = 4
TILES = 128
layer_eps = 1e-05
root_half = 0.7071067811865476
inv_root_two_pi = 0.3989422804014327
SCALE = 16.0 / math.sqrt(TILES * HALF * HALF)
PAY = 3 * D
LINK = f32
WIN = 256


def dot(left, right, dims=((1,), (0,))):
    return lax.dot_general(left, right, (dims, ((), ())), preferred_element_type=f32)


NT = ((1,), (1,))
TN = ((0,), (0,))


def iota(shape, dim):
    return lax.broadcasted_iota(jnp.int32, shape, dim)


def one_hot(cond):
    return jnp.where(cond, 1.0, 0.0).astype(bf16)


def split3(x):
    hi = x.astype(bf16)
    rest = x - hi.astype(f32)
    mid = rest.astype(bf16)
    lo = (rest - mid.astype(f32)).astype(bf16)
    return hi, mid, lo


def split2(x):
    hi = x.astype(bf16)
    return hi, (x - hi.astype(f32)).astype(bf16)


def feature_of(lane):
    return (lane // 128) * 8 + lane % 8


def main_kernel(
    lat_h, rew_h, cur_h, cnt_h, win_h, wv_h, wg_h, wd_h, wo_h,
    blend_o, g_o, p_o,
    lat_s, cnt_s, rew_v, cur_v, win_v, wv, wg, wd, wo_v,
    regf, cntf, x_s, hid_s, gel_s, vs_s, q_s, act_s,
    part_s, rs_send, rs_in, cot_in, blend_in, cot_mine, blend_mine, wdo_s, woe_s, wrep_s,
    pay_s, pay_send, pay_in, z_in, z_mine, g_in, ps_s, ps_send, ps_in, pz_in, pz_mine, p_in,
    lat_own, cnt_own, relay_sem, slab_sem,
    loc_sem, send_sem, halo_sem, rs_sem, cot_sem, blend_sem, pay_sem, z_sem, g_sem, ps_sem, pz_sem, p_sem,
):
    t = lax.axis_index("tile")
    p = lax.axis_index("mp")
    plane = t // 8
    member = t % 8
    base8 = plane * 8
    chip = t // 2
    k = t % 2
    across = t % 8 // 2
    odd = plane % 2

    def snake(row):
        z, r = row // 4, row % 4
        return 4 * z + jnp.where(z % 2 == 1, 3 - r, r)

    def shifted(row, n):
        return (row + n + GRID_ROWS) % GRID_ROWS

    grid_row = snake(chip)
    mirror = grid_row
    up_chip = snake(shifted(grid_row, -1))
    down_chip = snake(shifted(grid_row, 1))
    near_n = snake(shifted(chip, 2 * k - 1))
    beside = jnp.where(k == 0, up_chip, down_chip)
    in_place = odd == 0
    far_home = near_n == chip

    loads = []
    for n, (src, dst) in enumerate([
        (lat_h, lat_own), (cnt_h, cnt_own), (wd_h, wd), (wo_h, wo_v), (win_h, win_v), (wv_h, wv), (wg_h, wg),
    ]):
        copy = pltpu.make_async_copy(src, dst, loc_sem.at[n])
        copy.start()
        loads.append(copy)
    slab_loads = [pltpu.make_async_copy(rew_h, rew_v, loc_sem.at[7]), pltpu.make_async_copy(cur_h, cur_v, loc_sem.at[8])]

    @pl.when(in_place)
    def _():
        for copy in slab_loads:
            copy.start()

    own_chip = [((2 * chip + (k + dk) % 2), (p + dq) % MP, (k + dk) % 2) for dk in range(2) for dq in range(MP)][1:]
    group = [(base8 + (member + n) % 8, (member + n) % 8) for n in range(1, 8)]
    every = [
        (base8 + (member + n) % 8, (p + dq) % MP, ((member + n) % 8) * MP + (p + dq) % MP)
        for n in range(8) for dq in range(MP)
    ][1:]
    planes = [(((plane + n) % 8) * 8 + member, (plane + n) % 8) for n in range(1, 8)]

    def hello(sem, target):
        pl.semaphore_signal(sem, inc=1, device_id=target, device_id_type=MESH)

    sides = [(t, (p + 1) % MP), (t, (p + MP - 1) % MP)]
    levels = [(planes[0][0], p), (planes[6][0], p)]
    along = [(2 * up_chip + k, p), (2 * down_chip + k, p)]
    barrier = pltpu.get_barrier_semaphore()
    near = [(2 * mirror + 1 - k, p), (2 * near_n + 1 - k, p), (2 * mirror + 1 - k, p)]
    near += [(2 * chip + 1 - k, p)] + sides + levels + along
    near += [(2 * up_chip + 1 - k, p), (2 * down_chip + 1 - k, p)]
    for target in near:
        hello(barrier, target)
    maybe = [
        2 * mirror + k, 2 * near_n + k, 2 * mirror + k,
        2 * shifted(grid_row, -1) + 1, 2 * shifted(grid_row, 1),
    ]
    count = len(near)
    for target in maybe:
        @pl.when(target != t)
        def _():
            hello(barrier, (target, p))

        count = count + jnp.where(target != t, 1, 0)

    lane256 = iota((1, 256), 1)
    expand = one_hot(iota((F, 256), 0) == feature_of(iota((F, 256), 1)))
    tj_mask = (iota((HALF, 1, 256), 2) % 128) // 8 == iota((HALF, 1, 256), 0)

    for copy in loads[2:5]:
        copy.wait()
    woe = dot(wo_v[...], expand, TN).astype(bf16)
    woe_s[...] = woe
    wdo = dot(wd[...], woe)
    wdo_hi, wdo_lo = split2(wdo)
    wdo_s[0] = wdo_hi
    wdo_s[1] = wdo_lo
    win = win_v[...]
    wrep_s[...] = dot(expand, win, TN).astype(bf16)

    loads[0].wait()
    loads[1].wait()
    pl.semaphore_wait(barrier, count)
    sent = []

    def remote(src, dst, n, sem, target):
        return pltpu.make_async_remote_copy(
            src_ref=src, dst_ref=dst, send_sem=send_sem.at[n], recv_sem=sem,
            device_id=target, device_id_type=MESH,
        )

    def send(src, dst, sem, target):
        copy = remote(src, dst, len(sent), sem, target)
        copy.start()
        sent.append((None, copy))

    def send_if(cond, src, dst, sem, target):
        copy = remote(src, dst, len(sent), sem, target)

        @pl.when(cond)
        def _():
            copy.start()

        sent.append((cond, copy))

    def arrive(dst, sem):
        remote(dst, dst, 0, sem, (t, p)).wait_recv()

    far_slot = 3 * (1 - k)
    for chip_to, slot, home in ((near_n, far_slot, far_home), (mirror, 1 + k, in_place)):
        for n, (own, slots) in enumerate(((lat_own, lat_s), (cnt_own, cnt_s))):
            send(own, slots.at[slot], halo_sem.at[n, slot], (2 * chip_to + 1 - k, p))
            send_if(jnp.logical_not(home), own, slots.at[slot], halo_sem.at[n, slot], (2 * chip_to + k, p))

        @pl.when(home)
        def _():
            lat_s[slot] = lat_own[...]
            cnt_s[slot] = cnt_own[...]

    for n, (src, dst) in enumerate(((rew_h, rew_v), (cur_h, cur_v))):
        send_if(odd == 1, src, dst, slab_sem.at[n], (2 * mirror + k, p))

    def tell(step, targets):
        for target in targets:
            hello(relay_sem.at[step], target)

    def hear(step):
        pl.semaphore_wait(relay_sem.at[step], 2)

    tell(0, sides)
    tell(4, levels)

    def arrive_halo(slot):
        arrive(lat_s.at[slot], halo_sem.at[0, slot])
        arrive(cnt_s.at[slot], halo_sem.at[1, slot])

    arrive_halo(2 - k)
    for slot, remote_slot in (
        (1 + k, odd == 1),
        (0, 2 * shifted(grid_row, -1) + 1 != t),
        (3, 2 * shifted(grid_row, 1) != t),
    ):
        @pl.when(remote_slot)
        def _():
            arrive_halo(slot)

    hear(0)
    hear(4)
    tell(1, sides)
    tell(5, levels)

    for slot in range(4):
        slab = lat_s[slot].astype(f32)
        regf[SLAB * slot : SLAB * slot + SLAB, :] = jnp.where(k == 0, slab[:, 0:WIN], slab[:, COLS - WIN : COLS])
        cntf[SLAB * slot : SLAB * slot + SLAB, :] = cnt_s[slot].astype(f32)

    lane96 = iota((8, CELLS), 1)
    row_win = jnp.where(cntf[8:16, :] == 2.0, 1.0, 0.0)
    col_win = jnp.where(cntf[24:32, :] == 2.0, 1.0, 0.0)
    first_row = iota((8, CELLS), 0) == 0
    selects = []
    for j in range(2):
        c = 2 * k + j
        n_row = jnp.sum(jnp.where(lane96 == SPACING * c + 12, row_win, 0.0), axis=1, keepdims=True)
        n_row = jnp.sum(n_row, axis=0, keepdims=True)
        row = 16.0 - n_row
        row = jnp.where(grid_row == 0, 12.0, jnp.where(grid_row == GRID_ROWS - 1, 4.0, row))
        near = first_row & (lane96 >= SPACING * c - JITTER) & (lane96 < SPACING * c + JITTER)
        n_col = jnp.sum(jnp.where(near, col_win, 0.0), axis=1, keepdims=True)
        n_col = jnp.sum(n_col, axis=0, keepdims=True)
        col = (SPACING * c + JITTER).astype(f32) - n_col
        col = jnp.where(c == 0, 0.0, jnp.where(c == 3, float(CELLS - SIDE), col))
        m = iota((SIDE, REGION), 0)
        pick = (2 * (m % HALF) + m // HALF).astype(f32) + row
        sel_r = one_hot(iota((SIDE, REGION), 1).astype(f32) == pick)
        shift = CH * col - ((COLS - WIN) * k).astype(f32)
        sel_c = one_hot(iota((WIN, 128), 0).astype(f32) == iota((WIN, 128), 1).astype(f32) + shift)
        m = iota((REGION, 3 * SIDE), 1) % SIDE
        pick = (2 * (m % HALF) + m // HALF).astype(f32) + row
        put_r = one_hot(iota((REGION, 3 * SIDE), 0).astype(f32) == pick)
        selects.append((sel_r, sel_c, put_r))

    def patches_of(region):
        tiles = []
        for sel_r, sel_c, _ in selects:
            rows = dot(sel_r, region).astype(bf16)
            crop = dot(rows, sel_c)
            pair = jnp.concatenate([crop[:HALF], crop[HALF:]], axis=1)
            full = jnp.where(tj_mask, pair.reshape(1, HALF, 256), 0.0)
            tiles.append(full.reshape(HALF * HALF, 256))
        return jnp.concatenate(tiles, axis=0)

    xf = patches_of(regf[...].astype(bf16))
    x = xf.astype(bf16)
    x_s[...] = x
    hidden = dot(x, wrep_s[...]).astype(bf16)
    hid_s[...] = hidden
    values = hidden.astype(f32)
    center = values - jnp.mean(values, axis=-1, keepdims=True)
    variance = jnp.mean(center * center, axis=-1, keepdims=True)
    inv = lax.rsqrt(variance + layer_eps)
    unit = (center * inv).astype(bf16)

    loads[5].wait()
    loads[6].wait()
    value = dot(unit, wv[...])
    gate = dot(unit, wg[...])
    phi = 0.5 * (1.0 + lax.erf(gate * root_half))
    gel = gate * phi
    act = (value * gel).astype(bf16)
    act_s[...] = act
    gel_s[...] = gel
    slope = value * (phi + gate * jnp.exp(-0.5 * gate * gate) * inv_root_two_pi)
    vs_s[...] = slope
    q_s[...] = gel * value + slope * gate

    noise = dot(act, wdo_s[0]) + dot(act, wdo_s[1])
    own = dot(hid_s[...], woe_s[...])
    noise = noise + jnp.where(p == 0, own, 0.0)
    placed = None
    for j in range(2):
        block = noise[256 * j : 256 * j + 256].reshape(HALF, HALF, 256)
        crop = jnp.sum(jnp.where(tj_mask, block, 0.0), axis=0)
        stack = jnp.concatenate(
            [part[:, 128 * a : 128 * a + 128] for part in split3(crop) for a in range(2)], axis=0
        )
        wide = dot(stack, selects[j][1], NT).astype(bf16)
        term = dot(selects[j][2], wide)
        placed = term if placed is None else placed + term
    part_s[...] = placed
    for g in range(16):
        rs_send[g] = part_s[3 * g : 3 * g + 3, :]

    hear(1)
    hear(5)
    for dev, q, kk in own_chip:
        send(rs_send.at[4 + 4 * kk + q], rs_in.at[4 * k + p], rs_sem.at[4 * k + p], (dev, q))
    for q in range(MP):
        send(rs_send.at[q], rs_in.at[8 + 4 * k + p], rs_sem.at[8 + 4 * k + p], (2 * up_chip + 1, q))
        send(rs_send.at[12 + q], rs_in.at[8 + 4 * k + p], rs_sem.at[8 + 4 * k + p], (2 * down_chip, q))
    rs_in[4 * k + p] = rs_send[4 + 4 * k + p]

    tell(2, along)
    tell(6, levels)

    xi = xf * inv
    xi_hi, xi_lo = split2(xi)
    pt = dot(expand, x, NT).astype(bf16)
    pit = jnp.concatenate([dot(expand, xi_hi, NT).astype(bf16), dot(expand, xi_lo, NT).astype(bf16)], axis=0)

    @pl.when(in_place)
    def _():
        for copy in slab_loads:
            copy.wait()

    @pl.when(odd == 1)
    def _():
        arrive(rew_v, slab_sem.at[0])
        arrive(cur_v, slab_sem.at[1])

    spread = one_hot(iota((CELLS, COLS), 0) == iota((CELLS, COLS), 1) // CH)
    cover = dot(cnt_s[1 + k].astype(f32).astype(bf16), spread)
    rew = rew_v[...]
    cur = cur_v[...]

    def my_rows(slab):
        out = slab[0:3]
        for q in range(1, MP):
            out = jnp.where(p == q, slab[3 * q : 3 * q + 3], out)
        return out

    cover3 = my_rows(cover)
    rew3 = my_rows(rew)
    cur3 = my_rows(cur)

    for dev, q, kk in own_chip:
        arrive(rs_in.at[4 * kk + q], rs_sem.at[4 * kk + q])
    for slot in range(8, 16):
        arrive(rs_in.at[slot], rs_sem.at[slot])
    sums = []
    for kk in range(2):
        part = rs_in[4 * kk]
        for slot in [4 * kk + 1, 4 * kk + 2, 4 * kk + 3] + [8 + 4 * kk + q for q in range(MP)]:
            part = part + rs_in[slot]
        sums.append(part)
    left, right = sums
    total = jnp.concatenate([left[:, 0:128], left[:, 128:] + right[:, 0:128], right[:, 128:]], axis=1)
    blend3 = total / cover3
    cot3 = ((rew3 - cur3 * blend3) / cover3 * SCALE).astype(bf16).astype(f32)
    blend_mine[...] = blend3
    cot_mine[0] = cot3[:, 0:WIN]
    cot_mine[1] = cot3[:, COLS - WIN : COLS]
    for dev, q, kk in own_chip:
        send(cot_mine.at[kk], cot_in.at[4 + 4 * k + p], cot_sem.at[4 + 4 * k + p], (dev, q))
    slot = 12 * (1 - k) + p
    for kk in range(2):
        for q in range(MP):
            send(cot_mine.at[kk], cot_in.at[slot], cot_sem.at[slot], (2 * beside + kk, q))
    hear(2)
    hear(6)
    tell(3, along)
    cot_in[4 + 4 * k + p] = cot_mine[k]

    for dev, q, kk in own_chip:
        arrive(cot_in.at[4 + 4 * kk + q], cot_sem.at[4 + 4 * kk + q])
    for q in range(MP):
        arrive(cot_in.at[q], cot_sem.at[q])
        arrive(cot_in.at[12 + q], cot_sem.at[12 + q])
    hear(3)
    for dq in range(1, MP):
        send(blend_mine, blend_in.at[p], blend_sem.at[p], (2 * mirror + k, (p + dq) % MP))
    send_if(odd == 1, blend_mine, blend_in.at[p], blend_sem.at[p], (2 * mirror + k, p))

    @pl.when(in_place)
    def _():
        blend_in[p] = blend_mine[...]

    for g in range(16):
        regf[3 * g : 3 * g + 3, :] = cot_in[g]

    y = patches_of(regf[...].astype(bf16)).astype(bf16)
    dfb = dot(y, woe_s[...], NT).astype(bf16)
    d_act = dot(dfb, wd[...], NT)
    dv = (d_act * gel_s[...]).astype(bf16)
    dg = (d_act * vs_s[...]).astype(bf16)
    ct = dot(expand, y, NT).astype(bf16)
    gv = dot(pit, dv)
    gg = dot(pit, dg)
    gv = gv[:F] + gv[F:]
    gg = gg[:F] + gg[F:]
    gd = dot(ct, act_s[...])
    pay_s[:, 0:D] = gv
    pay_s[:, D : 2 * D] = gg
    pay_s[:, 2 * D : 3 * D] = gd
    for c in range(8):
        pay_send[c] = pay_s[2 * c : 2 * c + 2, :].astype(pay_send.dtype)

    for dev, c in group:
        send(pay_send.at[c], pay_in.at[member], pay_sem.at[member], (dev, p))
    pay_in[member] = pay_send[member]

    def rows_dot(piece, right, dims=((1,), (0,))):
        both = dot(jnp.concatenate(split2(piece), axis=0), right, dims)
        return both[:F] + both[F:]

    m2 = jnp.sum(d_act * q_s[...], axis=1, keepdims=True) * (1.0 / D)
    xm_hi, xm_lo = split2(xi * m2)
    b_w = dot(pit, xm_hi) + dot(pit, xm_lo)
    b_w = b_w[:F] + b_w[F:]
    inner = rows_dot(gv, wv[...], NT) + rows_dot(gg, wg[...], NT) - rows_dot(b_w, wrep_s[...])
    inner = inner - jnp.mean(inner, axis=1, keepdims=True)
    ps_s[0:F, :] = inner + 0.25 * rows_dot(dot(pt, y), woe_s[...], NT)
    ps_s[F : 2 * F, :] = rows_dot(gd, wd[...]) + 0.25 * rows_dot(dot(ct, x_s[...]), wrep_s[...])
    for n in range(2 * F):
        ps_send[n] = ps_s[n : n + 1, :]
    mine = MP * member + p
    for dev, q, n in every:
        send(ps_send.at[n], ps_in.at[mine], ps_sem.at[mine], (dev, q))
    ps_in[mine] = ps_send[mine]

    for dev, c in group:
        arrive(pay_in.at[c], pay_sem.at[c])
    rows = pay_in[0].astype(f32)
    for c in range(1, 8):
        rows = rows + pay_in[c].astype(f32)
    z_mine[...] = rows.astype(z_mine.dtype)
    for dev, c in planes:
        send(z_mine, z_in.at[plane], z_sem.at[plane], (dev, p))
    z_in[plane] = z_mine[...]

    for dev, q, n in every:
        arrive(ps_in.at[n], ps_sem.at[n])
    row = ps_in[0]
    for n in range(1, 2 * F):
        row = row + ps_in[n]
    pz_mine[...] = row
    for dev, c in planes:
        send(pz_mine, pz_in.at[plane], pz_sem.at[plane], (dev, p))
    pz_in[plane] = row

    for dev, c in planes:
        arrive(z_in.at[c], z_sem.at[c])
    rows = z_in[0].astype(f32)
    for c in range(1, 8):
        rows = rows + z_in[c].astype(f32)
    g_in[member] = rows
    for dev, c in group:
        send(g_in.at[member], g_in.at[member], g_sem.at[member], (dev, p))

    for dev, c in planes:
        arrive(pz_in.at[c], pz_sem.at[c])
    row = pz_in[0]
    for c in range(1, 8):
        row = row + pz_in[c]
    p_in[mine] = row
    for dev, q, n in every:
        send(p_in.at[mine], p_in.at[mine], p_sem.at[mine], (dev, q))

    for dq in range(1, MP):
        q = (p + dq) % MP
        arrive(blend_in.at[q], blend_sem.at[q])

    @pl.when(odd == 1)
    def _():
        arrive(blend_in.at[p], blend_sem.at[p])

    for q in range(MP):
        blend_o[3 * q : 3 * q + 3, :] = blend_in[q]
    for dev, c in group:
        arrive(g_in.at[c], g_sem.at[c])
    for c in range(8):
        g_o[2 * c : 2 * c + 2, :] = g_in[c]
    for dev, q, n in every:
        arrive(p_in.at[n], p_sem.at[n])
    for n in range(2 * F):
        p_o[n : n + 1, :] = p_in[n]
    for cond, copy in sent:
        if cond is None:
            copy.wait_send()
        else:
            pl.when(cond)(copy.wait_send)

def final_kernel(blend, g, both, win, wo, blend_o, gin_o, gv_o, gg_o, gd_o, gout_o, out_s, out_sem):
    w = win[...]
    w3 = jnp.concatenate([w, w, w], axis=0)
    mean = jnp.mean(w.astype(f32), axis=1, keepdims=True)
    wot = wo[...]
    wot3 = jnp.concatenate([wot, wot, wot], axis=0)
    half = D // 2
    copies = []
    for n, out in enumerate((gv_o, gg_o, gd_o)):
        rows = g[:, D * n : D * n + D]
        stack = jnp.concatenate(split3(rows), axis=0)
        left, right = (w3, stack) if n < 2 else (stack, wot3)
        for h in range(2):
            block = dot(left[:, half * h : half * h + half], right, TN)
            if n < 2:
                block = block - jnp.sum(mean * rows, axis=0, keepdims=True)
            out_s[n, half * h : half * h + half, :] = block
            copy = pltpu.make_async_copy(
                out_s.at[n, pl.ds(half * h, half)], out.at[pl.ds(half * h, half)], out_sem.at[2 * n + h]
            )
            copy.start()
            copies.append(copy)
    blend_o[...] = blend[...]
    gin_o[...] = both[0:F, :]
    gout_o[...] = both[F : 2 * F, :]
    for copy in copies:
        copy.wait()


def per_device(latent, reward_grad, curvature, offsets, counts, w_in, w_value, w_gate, w_down, w_out):
    vm = pltpu.VMEM
    any_spec = pl.BlockSpec(memory_space=pl.ANY)
    vm_spec = pl.BlockSpec(memory_space=pltpu.VMEM)
    tokens = 2 * HALF * HALF
    dma = pltpu.SemaphoreType.DMA
    scratch = [
        vm((4, SLAB, COLS), bf16), vm((4, SLAB, CELLS), jnp.int32), vm((SLAB, COLS), f32), vm((SLAB, COLS), f32),
        vm((F, D), bf16), vm((D, D), bf16), vm((D, D), bf16), vm((D, D), bf16), vm((F, D), bf16),
        vm((REGION, WIN), f32), vm((REGION, CELLS), f32), vm((tokens, 256), bf16), vm((tokens, D), bf16),
        vm((tokens, D), f32), vm((tokens, D), f32), vm((tokens, D), f32), vm((tokens, D), bf16),
        vm((REGION, WIN), f32), vm((16, 3, WIN), f32), vm((16, 3, WIN), f32), vm((16, 3, WIN), f32),
        vm((MP, 3, COLS), f32), vm((2, 3, WIN), f32), vm((3, COLS), f32), vm((2, D, 256), bf16), vm((D, 256), bf16),
        vm((256, D), bf16),
        vm((F, PAY), f32), vm((8, 2, PAY), LINK), vm((8, 2, PAY), LINK), vm((8, 2, PAY), LINK), vm((2, PAY), LINK),
        vm((8, 2, PAY), f32), vm((2 * F, D), f32), vm((2 * F, 1, D), f32), vm((2 * F, 1, D), f32), vm((8, 1, D), f32),
        vm((1, D), f32), vm((2 * F, 1, D), f32),
        vm((SLAB, COLS), bf16), vm((SLAB, CELLS), jnp.int32), pltpu.SemaphoreType.REGULAR((7,)), dma((2,)),
        dma((9,)), dma((136,)), dma((2, 4)), dma((16,)), dma((16,)), dma((MP,)), dma((8,)), dma((8,)), dma((8,)),
        dma((2 * F,)), dma((8,)), dma((2 * F,)),
    ]
    sds = jax.ShapeDtypeStruct
    blend, g, both = pl.pallas_call(
        main_kernel,
        out_shape=(sds((SLAB, COLS), f32), sds((F, 3 * D), f32), sds((2 * F, D), f32)),
        in_specs=[any_spec] * 9,
        out_specs=(vm_spec,) * 3,
        scratch_shapes=scratch,
        compiler_params=pltpu.CompilerParams(
            collective_id=0, has_side_effects=True, vmem_limit_bytes=56 * 1024 * 1024
        ),
        name="tile_gradients",
    )(latent, reward_grad, curvature, counts, w_in, w_value, w_gate, w_down, w_out.T)
    *outs, grad_out = pl.pallas_call(
        final_kernel,
        out_shape=(
            sds((SLAB, COLS), f32), sds((F, D), f32), sds((D, D), f32), sds((D, D), f32), sds((D, D), f32),
            sds((F, D), f32),
        ),
        in_specs=[vm_spec] * 5,
        out_specs=(vm_spec, vm_spec, any_spec, any_spec, any_spec, vm_spec),
        scratch_shapes=[vm((3, D, D), f32), dma((6,))],
        name="weight_outputs",
    )(blend, g, both, w_in, w_out.T)
    return (*outs, grad_out.T)


def solution(mesh):
    return jax.shard_map(
        per_device,
        mesh=mesh,
        in_specs=(
            P("tile", None), P("tile", None), P("tile", None), P("tile", None), P("tile", None), P(),
            P(None, "mp"), P(None, "mp"), P("mp", None), P(),
        ),
        out_specs=(P("tile", None), P(), P(None, "mp"), P(None, "mp"), P("mp", None), P()),
        check_vma=False,
    )
```

```python
import functools
import math

import jax
import jax.numpy as jnp
from jax import lax
from jax.experimental import pallas as pl
from jax.experimental.pallas import tpu as pltpu
from jax.sharding import PartitionSpec as P

MESH = pl.DeviceIdType.MESH
bf16 = jnp.bfloat16
f32 = jnp.float32

SIDE = 32
HALF = 16
SPACING = 24
JITTER = 4
CH = 4
F = 16
D = 640
COLS = 384
CELLS = 96
SLAB = 12
REGION = 48
GRID_ROWS = 32
MP = 4
TILES = 128
layer_eps = 1e-05
root_half = 0.7071067811865476
inv_root_two_pi = 0.3989422804014327
SCALE = 16.0 / math.sqrt(TILES * HALF * HALF)
PAY = 3 * D
LINK = bf16
WIN = 256


def dot(left, right, dims=((1,), (0,))):
    return lax.dot_general(left, right, (dims, ((), ())), preferred_element_type=f32)


NT = ((1,), (1,))
TN = ((0,), (0,))


def iota(shape, dim):
    return lax.broadcasted_iota(jnp.int32, shape, dim)


def one_hot(cond):
    return jnp.where(cond, 1.0, 0.0).astype(bf16)


def split3(x):
    hi = x.astype(bf16)
    rest = x - hi.astype(f32)
    mid = rest.astype(bf16)
    lo = (rest - mid.astype(f32)).astype(bf16)
    return hi, mid, lo


def split2(x):
    hi = x.astype(bf16)
    return hi, (x - hi.astype(f32)).astype(bf16)


def feature_of(lane):
    return (lane // 128) * 8 + lane % 8


def main_kernel(
    lat_h, rew_h, cur_h, cnt_h, win_h, wv_h, wg_h, wd_h, wo_h,
    blend_o, g_o, p_o,
    lat_s, cnt_s, rew_v, cur_v, win_v, wv, wg, wd, wo_v,
    regf, cntf, x_s, hid_s, gel_s, vs_s, q_s, act_s,
    part_s, rs_send, rs_in, cot_in, blend_in, cot_mine, blend_mine, wdo_s, woe_s, wrep_s,
    pay_s, pay_send, pay_in, z_in, z_mine, g_in, ps_s, ps_send, ps_in, pz_in, pz_mine, p_in,
    lat_own, cnt_own, relay_sem, slab_sem,
    loc_sem, send_sem, halo_sem, rs_sem, cot_sem, blend_sem, pay_sem, z_sem, g_sem, ps_sem, pz_sem, p_sem,
):
    t = lax.axis_index("tile")
    p = lax.axis_index("mp")
    plane = t // 8
    member = t % 8
    base8 = plane * 8
    chip = t // 2
    k = t % 2
    across = t % 8 // 2
    odd = plane % 2

    def snake(row):
        z, r = row // 4, row % 4
        return 4 * z + jnp.where(z % 2 == 1, 3 - r, r)

    def shifted(row, n):
        return (row + n + GRID_ROWS) % GRID_ROWS

    grid_row = snake(chip)
    mirror = grid_row
    up_chip = snake(shifted(grid_row, -1))
    down_chip = snake(shifted(grid_row, 1))
    near_n = snake(shifted(chip, 2 * k - 1))
    beside = jnp.where(k == 0, up_chip, down_chip)
    in_place = odd == 0
    far_home = near_n == chip

    loads = []
    for n, (src, dst) in enumerate([
        (lat_h, lat_own), (cnt_h, cnt_own), (wd_h, wd), (wo_h, wo_v), (win_h, win_v), (wv_h, wv), (wg_h, wg),
    ]):
        copy = pltpu.make_async_copy(src, dst, loc_sem.at[n])
        copy.start()
        loads.append(copy)
    slab_loads = [pltpu.make_async_copy(rew_h, rew_v, loc_sem.at[7]), pltpu.make_async_copy(cur_h, cur_v, loc_sem.at[8])]

    @pl.when(in_place)
    def _():
        for copy in slab_loads:
            copy.start()

    own_chip = [((2 * chip + (k + dk) % 2), (p + dq) % MP, (k + dk) % 2) for dk in range(2) for dq in range(MP)][1:]
    group = [(base8 + (member + n) % 8, (member + n) % 8) for n in range(1, 8)]
    every = [
        (base8 + (member + n) % 8, (p + dq) % MP, ((member + n) % 8) * MP + (p + dq) % MP)
        for n in range(8) for dq in range(MP)
    ][1:]
    planes = [(((plane + n) % 8) * 8 + member, (plane + n) % 8) for n in range(1, 8)]

    def hello(sem, target):
        pl.semaphore_signal(sem, inc=1, device_id=target, device_id_type=MESH)

    sides = [(t, (p + 1) % MP), (t, (p + MP - 1) % MP)]
    levels = [(planes[0][0], p), (planes[6][0], p)]
    along = [(2 * up_chip + k, p), (2 * down_chip + k, p)]
    barrier = pltpu.get_barrier_semaphore()
    near = [(2 * mirror + 1 - k, p), (2 * near_n + 1 - k, p), (2 * mirror + 1 - k, p)]
    near += [(2 * chip + 1 - k, p)] + sides + levels + along
    near += [(2 * up_chip + 1 - k, p), (2 * down_chip + 1 - k, p)]
    for target in near:
        hello(barrier, target)
    maybe = [
        2 * mirror + k, 2 * near_n + k, 2 * mirror + k,
        2 * shifted(grid_row, -1) + 1, 2 * shifted(grid_row, 1),
    ]
    count = len(near)
    for target in maybe:
        @pl.when(target != t)
        def _():
            hello(barrier, (target, p))

        count = count + jnp.where(target != t, 1, 0)

    loads[0].wait()
    loads[1].wait()
    pl.semaphore_wait(barrier, count)
    sent = []

    def remote(src, dst, n, sem, target):
        return pltpu.make_async_remote_copy(
            src_ref=src, dst_ref=dst, send_sem=send_sem.at[n], recv_sem=sem,
            device_id=target, device_id_type=MESH,
        )

    def send(src, dst, sem, target):
        copy = remote(src, dst, len(sent), sem, target)
        copy.start()
        sent.append((None, copy))

    def send_if(cond, src, dst, sem, target):
        copy = remote(src, dst, len(sent), sem, target)

        @pl.when(cond)
        def _():
            copy.start()

        sent.append((cond, copy))

    def arrive(dst, sem):
        remote(dst, dst, 0, sem, (t, p)).wait_recv()

    far_slot = 3 * (1 - k)
    for chip_to, slot, home in ((near_n, far_slot, far_home), (mirror, 1 + k, in_place)):
        for n, (own, slots) in enumerate(((lat_own, lat_s), (cnt_own, cnt_s))):
            send(own, slots.at[slot], halo_sem.at[n, slot], (2 * chip_to + 1 - k, p))
            send_if(jnp.logical_not(home), own, slots.at[slot], halo_sem.at[n, slot], (2 * chip_to + k, p))

        @pl.when(home)
        def _():
            lat_s[slot] = lat_own[...]
            cnt_s[slot] = cnt_own[...]

    for n, (src, dst) in enumerate(((rew_h, rew_v), (cur_h, cur_v))):
        send_if(odd == 1, src, dst, slab_sem.at[n], (2 * mirror + k, p))

    def tell(step, targets):
        for target in targets:
            hello(relay_sem.at[step], target)

    def hear(step):
        pl.semaphore_wait(relay_sem.at[step], 2)

    tell(0, sides)
    tell(4, levels)

    lane256 = iota((1, 256), 1)
    expand = one_hot(iota((F, 256), 0) == feature_of(iota((F, 256), 1)))
    tj_mask = (iota((HALF, 1, 256), 2) % 128) // 8 == iota((HALF, 1, 256), 0)

    for copy in loads[2:5]:
        copy.wait()
    woe = dot(wo_v[...], expand, TN).astype(bf16)
    woe_s[...] = woe
    wdo = dot(wd[...], woe)
    wdo_hi, wdo_lo = split2(wdo)
    wdo_s[0] = wdo_hi
    wdo_s[1] = wdo_lo
    win = win_v[...]
    wrep_s[...] = dot(expand, win, TN).astype(bf16)

    def arrive_halo(slot):
        arrive(lat_s.at[slot], halo_sem.at[0, slot])
        arrive(cnt_s.at[slot], halo_sem.at[1, slot])

    arrive_halo(2 - k)
    for slot, remote_slot in (
        (1 + k, odd == 1),
        (0, 2 * shifted(grid_row, -1) + 1 != t),
        (3, 2 * shifted(grid_row, 1) != t),
    ):
        @pl.when(remote_slot)
        def _():
            arrive_halo(slot)

    hear(0)
    hear(4)
    tell(1, sides)
    tell(5, levels)

    for slot in range(4):
        slab = lat_s[slot].astype(f32)
        regf[SLAB * slot : SLAB * slot + SLAB, :] = jnp.where(k == 0, slab[:, 0:WIN], slab[:, COLS - WIN : COLS])
        cntf[SLAB * slot : SLAB * slot + SLAB, :] = cnt_s[slot].astype(f32)

    lane96 = iota((8, CELLS), 1)
    row_win = jnp.where(cntf[8:16, :] == 2.0, 1.0, 0.0)
    col_win = jnp.where(cntf[24:32, :] == 2.0, 1.0, 0.0)
    first_row = iota((8, CELLS), 0) == 0
    selects = []
    for j in range(2):
        c = 2 * k + j
        n_row = jnp.sum(jnp.where(lane96 == SPACING * c + 12, row_win, 0.0), axis=1, keepdims=True)
        n_row = jnp.sum(n_row, axis=0, keepdims=True)
        row = 16.0 - n_row
        row = jnp.where(grid_row == 0, 12.0, jnp.where(grid_row == GRID_ROWS - 1, 4.0, row))
        near = first_row & (lane96 >= SPACING * c - JITTER) & (lane96 < SPACING * c + JITTER)
        n_col = jnp.sum(jnp.where(near, col_win, 0.0), axis=1, keepdims=True)
        n_col = jnp.sum(n_col, axis=0, keepdims=True)
        col = (SPACING * c + JITTER).astype(f32) - n_col
        col = jnp.where(c == 0, 0.0, jnp.where(c == 3, float(CELLS - SIDE), col))
        m = iota((SIDE, REGION), 0)
        pick = (2 * (m % HALF) + m // HALF).astype(f32) + row
        sel_r = one_hot(iota((SIDE, REGION), 1).astype(f32) == pick)
        shift = CH * col - ((COLS - WIN) * k).astype(f32)
        sel_c = one_hot(iota((WIN, 128), 0).astype(f32) == iota((WIN, 128), 1).astype(f32) + shift)
        m = iota((REGION, 3 * SIDE), 1) % SIDE
        pick = (2 * (m % HALF) + m // HALF).astype(f32) + row
        put_r = one_hot(iota((REGION, 3 * SIDE), 0).astype(f32) == pick)
        selects.append((sel_r, sel_c, put_r))

    def patches_of(region):
        tiles = []
        for sel_r, sel_c, _ in selects:
            rows = dot(sel_r, region).astype(bf16)
            crop = dot(rows, sel_c)
            pair = jnp.concatenate([crop[:HALF], crop[HALF:]], axis=1)
            full = jnp.where(tj_mask, pair.reshape(1, HALF, 256), 0.0)
            tiles.append(full.reshape(HALF * HALF, 256))
        return jnp.concatenate(tiles, axis=0)

    xf = patches_of(regf[...].astype(bf16))
    x = xf.astype(bf16)
    x_s[...] = x
    hidden = dot(x, wrep_s[...]).astype(bf16)
    hid_s[...] = hidden
    values = hidden.astype(f32)
    center = values - jnp.mean(values, axis=-1, keepdims=True)
    variance = jnp.mean(center * center, axis=-1, keepdims=True)
    inv = lax.rsqrt(variance + layer_eps)
    unit = (center * inv).astype(bf16)

    loads[5].wait()
    loads[6].wait()
    value = dot(unit, wv[...])
    gate = dot(unit, wg[...])
    phi = 0.5 * (1.0 + lax.erf(gate * root_half))
    gel = gate * phi
    act = (value * gel).astype(bf16)
    act_s[...] = act
    gel_s[...] = gel
    slope = value * (phi + gate * jnp.exp(-0.5 * gate * gate) * inv_root_two_pi)
    vs_s[...] = slope
    q_s[...] = gel * value + slope * gate

    noise = dot(act, wdo_s[0]) + dot(act, wdo_s[1])
    own = dot(hid_s[...], woe_s[...])
    noise = noise + jnp.where(p == 0, own, 0.0)
    placed = None
    for j in range(2):
        block = noise[256 * j : 256 * j + 256].reshape(HALF, HALF, 256)
        crop = jnp.sum(jnp.where(tj_mask, block, 0.0), axis=0)
        stack = jnp.concatenate(
            [part[:, 128 * a : 128 * a + 128] for part in split3(crop) for a in range(2)], axis=0
        )
        wide = dot(stack, selects[j][1], NT).astype(bf16)
        term = dot(selects[j][2], wide)
        placed = term if placed is None else placed + term
    part_s[...] = placed
    for g in range(16):
        rs_send[g] = part_s[3 * g : 3 * g + 3, :]

    hear(1)
    hear(5)
    for dev, q, kk in own_chip:
        send(rs_send.at[4 + 4 * kk + q], rs_in.at[4 * k + p], rs_sem.at[4 * k + p], (dev, q))
    for q in range(MP):
        send(rs_send.at[q], rs_in.at[8 + 4 * k + p], rs_sem.at[8 + 4 * k + p], (2 * up_chip + 1, q))
        send(rs_send.at[12 + q], rs_in.at[8 + 4 * k + p], rs_sem.at[8 + 4 * k + p], (2 * down_chip, q))
    rs_in[4 * k + p] = rs_send[4 + 4 * k + p]

    tell(2, along)
    tell(6, levels)

    xi = xf * inv
    xi_hi, xi_lo = split2(xi)
    pt = dot(expand, x, NT).astype(bf16)
    pit = jnp.concatenate([dot(expand, xi_hi, NT).astype(bf16), dot(expand, xi_lo, NT).astype(bf16)], axis=0)

    @pl.when(in_place)
    def _():
        for copy in slab_loads:
            copy.wait()

    @pl.when(odd == 1)
    def _():
        arrive(rew_v, slab_sem.at[0])
        arrive(cur_v, slab_sem.at[1])

    spread = one_hot(iota((CELLS, COLS), 0) == iota((CELLS, COLS), 1) // CH)
    cover = dot(cnt_s[1 + k].astype(f32).astype(bf16), spread)
    rew = rew_v[...]
    cur = cur_v[...]

    def my_rows(slab):
        out = slab[0:3]
        for q in range(1, MP):
            out = jnp.where(p == q, slab[3 * q : 3 * q + 3], out)
        return out

    cover3 = my_rows(cover)
    rew3 = my_rows(rew)
    cur3 = my_rows(cur)

    for dev, q, kk in own_chip:
        arrive(rs_in.at[4 * kk + q], rs_sem.at[4 * kk + q])
    for slot in range(8, 16):
        arrive(rs_in.at[slot], rs_sem.at[slot])
    sums = []
    for kk in range(2):
        part = rs_in[4 * kk]
        for slot in [4 * kk + 1, 4 * kk + 2, 4 * kk + 3] + [8 + 4 * kk + q for q in range(MP)]:
            part = part + rs_in[slot]
        sums.append(part)
    left, right = sums
    total = jnp.concatenate([left[:, 0:128], left[:, 128:] + right[:, 0:128], right[:, 128:]], axis=1)
    blend3 = total / cover3
    cot3 = ((rew3 - cur3 * blend3) / cover3 * SCALE).astype(bf16).astype(f32)
    blend_mine[...] = blend3
    cot_mine[0] = cot3[:, 0:WIN]
    cot_mine[1] = cot3[:, COLS - WIN : COLS]
    for dev, q, kk in own_chip:
        send(cot_mine.at[kk], cot_in.at[4 + 4 * k + p], cot_sem.at[4 + 4 * k + p], (dev, q))
    slot = 12 * (1 - k) + p
    for kk in range(2):
        for q in range(MP):
            send(cot_mine.at[kk], cot_in.at[slot], cot_sem.at[slot], (2 * beside + kk, q))
    hear(2)
    hear(6)
    tell(3, along)
    cot_in[4 + 4 * k + p] = cot_mine[k]

    for dev, q, kk in own_chip:
        arrive(cot_in.at[4 + 4 * kk + q], cot_sem.at[4 + 4 * kk + q])
    for q in range(MP):
        arrive(cot_in.at[q], cot_sem.at[q])
        arrive(cot_in.at[12 + q], cot_sem.at[12 + q])
    hear(3)
    for dq in range(1, MP):
        send(blend_mine, blend_in.at[p], blend_sem.at[p], (2 * mirror + k, (p + dq) % MP))
    send_if(odd == 1, blend_mine, blend_in.at[p], blend_sem.at[p], (2 * mirror + k, p))

    @pl.when(in_place)
    def _():
        blend_in[p] = blend_mine[...]

    for g in range(16):
        regf[3 * g : 3 * g + 3, :] = cot_in[g]

    y = patches_of(regf[...].astype(bf16)).astype(bf16)
    dfb = dot(y, woe_s[...], NT).astype(bf16)
    d_act = dot(dfb, wd[...], NT)
    dv = (d_act * gel_s[...]).astype(bf16)
    dg = (d_act * vs_s[...]).astype(bf16)
    ct = dot(expand, y, NT).astype(bf16)
    gv = dot(pit, dv)
    gg = dot(pit, dg)
    gv = gv[:F] + gv[F:]
    gg = gg[:F] + gg[F:]
    gd = dot(ct, act_s[...])
    pay_s[:, 0:D] = gv
    pay_s[:, D : 2 * D] = gg
    pay_s[:, 2 * D : 3 * D] = gd
    for c in range(8):
        pay_send[c] = pay_s[2 * c : 2 * c + 2, :].astype(pay_send.dtype)

    for dev, c in group:
        send(pay_send.at[c], pay_in.at[member], pay_sem.at[member], (dev, p))
    pay_in[member] = pay_send[member]

    def rows_dot(piece, right, dims=((1,), (0,))):
        both = dot(jnp.concatenate(split2(piece), axis=0), right, dims)
        return both[:F] + both[F:]

    m2 = jnp.sum(d_act * q_s[...], axis=1, keepdims=True) * (1.0 / D)
    xm_hi, xm_lo = split2(xi * m2)
    b_w = dot(pit, xm_hi) + dot(pit, xm_lo)
    b_w = b_w[:F] + b_w[F:]
    inner = rows_dot(gv, wv[...], NT) + rows_dot(gg, wg[...], NT) - rows_dot(b_w, wrep_s[...])
    inner = inner - jnp.mean(inner, axis=1, keepdims=True)
    ps_s[0:F, :] = inner + 0.25 * rows_dot(dot(pt, y), woe_s[...], NT)
    ps_s[F : 2 * F, :] = rows_dot(gd, wd[...]) + 0.25 * rows_dot(dot(ct, x_s[...]), wrep_s[...])
    for n in range(2 * F):
        ps_send[n] = ps_s[n : n + 1, :]
    mine = MP * member + p
    for dev, q, n in every:
        send(ps_send.at[n], ps_in.at[mine], ps_sem.at[mine], (dev, q))
    ps_in[mine] = ps_send[mine]

    for dev, c in group:
        arrive(pay_in.at[c], pay_sem.at[c])
    rows = pay_in[0].astype(f32)
    for c in range(1, 8):
        rows = rows + pay_in[c].astype(f32)
    z_mine[...] = rows.astype(z_mine.dtype)
    for dev, c in planes:
        send(z_mine, z_in.at[plane], z_sem.at[plane], (dev, p))
    z_in[plane] = z_mine[...]

    for dev, q, n in every:
        arrive(ps_in.at[n], ps_sem.at[n])
    row = ps_in[0]
    for n in range(1, 2 * F):
        row = row + ps_in[n]
    pz_mine[...] = row
    for dev, c in planes:
        send(pz_mine, pz_in.at[plane], pz_sem.at[plane], (dev, p))
    pz_in[plane] = row

    for dev, c in planes:
        arrive(z_in.at[c], z_sem.at[c])
    rows = z_in[0].astype(f32)
    for c in range(1, 8):
        rows = rows + z_in[c].astype(f32)
    g_in[member] = rows
    for dev, c in group:
        send(g_in.at[member], g_in.at[member], g_sem.at[member], (dev, p))

    for dev, c in planes:
        arrive(pz_in.at[c], pz_sem.at[c])
    row = pz_in[0]
    for c in range(1, 8):
        row = row + pz_in[c]
    p_in[mine] = row
    for dev, q, n in every:
        send(p_in.at[mine], p_in.at[mine], p_sem.at[mine], (dev, q))

    for dq in range(1, MP):
        q = (p + dq) % MP
        arrive(blend_in.at[q], blend_sem.at[q])

    @pl.when(odd == 1)
    def _():
        arrive(blend_in.at[p], blend_sem.at[p])

    outs = [(blend_in, blend_o), (g_in, g_o), (p_in, p_o)]
    outs = [pltpu.make_async_copy(src, dst, loc_sem.at[9 + n]) for n, (src, dst) in enumerate(outs)]
    outs[0].start()
    for dev, c in group:
        arrive(g_in.at[c], g_sem.at[c])
    outs[1].start()
    for dev, q, n in every:
        arrive(p_in.at[n], p_sem.at[n])
    outs[2].start()
    for cond, copy in sent:
        if cond is None:
            copy.wait_send()
        else:
            pl.when(cond)(copy.wait_send)
    for copy in outs:
        copy.wait()

def final_kernel(
    blend_h, g_h, both_h, win_h, wo_h, blend_o, gin_o, gv_o, gg_o, gd_o, gout_o,
    blend_v, g_v, both_v, win_v, wo_v, g, blend_s, both_s, out_s, in_sem, out_sem,
):
    loads = [
        pltpu.make_async_copy(src, dst, in_sem.at[n])
        for n, (src, dst) in enumerate(
            ((g_h, g_v), (win_h, win_v), (wo_h, wo_v), (blend_h, blend_v), (both_h, both_v))
        )
    ]
    for copy in loads:
        copy.start()
    for copy in loads[:3]:
        copy.wait()
    for c in range(8):
        g[2 * c : 2 * c + 2, :] = g_v[c]
    w = win_v[...]
    w3 = jnp.concatenate([w, w, w], axis=0)
    mean = jnp.mean(w.astype(f32), axis=1, keepdims=True)
    wot = wo_v[...]
    wot3 = jnp.concatenate([wot, wot, wot], axis=0)
    half = D // 2
    copies = []

    def put(src, dst):
        copy = pltpu.make_async_copy(src, dst, out_sem.at[len(copies)])
        copy.start()
        copies.append(copy)

    for n, out in enumerate((gv_o, gg_o, gd_o)):
        rows = g[:, D * n : D * n + D]
        stack = jnp.concatenate(split3(rows), axis=0)
        left, right = (w3, stack) if n < 2 else (stack, wot3)
        for h in range(2):
            block = dot(left[:, half * h : half * h + half], right, TN)
            if n < 2:
                block = block - jnp.sum(mean * rows, axis=0, keepdims=True)
            out_s[n, half * h : half * h + half, :] = block
            put(out_s.at[n, pl.ds(half * h, half)], out.at[pl.ds(half * h, half)])
    for copy in loads[3:]:
        copy.wait()
    for q in range(MP):
        blend_s[3 * q : 3 * q + 3, :] = blend_v[q]
    for n in range(2 * F):
        both_s[n : n + 1, :] = both_v[n]
    put(blend_s, blend_o)
    put(both_s.at[0:F], gin_o)
    put(both_s.at[F : 2 * F], gout_o)
    for copy in copies:
        copy.wait()


def per_device(latent, reward_grad, curvature, offsets, counts, w_in, w_value, w_gate, w_down, w_out):
    vm = pltpu.VMEM
    any_spec = pl.BlockSpec(memory_space=pl.ANY)
    tokens = 2 * HALF * HALF
    dma = pltpu.SemaphoreType.DMA
    scratch = [
        vm((4, SLAB, COLS), bf16), vm((4, SLAB, CELLS), jnp.int32), vm((SLAB, COLS), f32), vm((SLAB, COLS), f32),
        vm((F, D), bf16), vm((D, D), bf16), vm((D, D), bf16), vm((D, D), bf16), vm((F, D), bf16),
        vm((REGION, WIN), f32), vm((REGION, CELLS), f32), vm((tokens, 256), bf16), vm((tokens, D), bf16),
        vm((tokens, D), f32), vm((tokens, D), f32), vm((tokens, D), f32), vm((tokens, D), bf16),
        vm((REGION, WIN), f32), vm((16, 3, WIN), f32), vm((16, 3, WIN), f32), vm((16, 3, WIN), f32),
        vm((MP, 3, COLS), f32), vm((2, 3, WIN), f32), vm((3, COLS), f32), vm((2, D, 256), bf16), vm((D, 256), bf16),
        vm((256, D), bf16),
        vm((F, PAY), f32), vm((8, 2, PAY), LINK), vm((8, 2, PAY), LINK), vm((8, 2, PAY), LINK), vm((2, PAY), LINK),
        vm((8, 2, PAY), f32), vm((2 * F, D), f32), vm((2 * F, 1, D), f32), vm((2 * F, 1, D), f32), vm((8, 1, D), f32),
        vm((1, D), f32), vm((2 * F, 1, D), f32),
        vm((SLAB, COLS), bf16), vm((SLAB, CELLS), jnp.int32), pltpu.SemaphoreType.REGULAR((7,)), dma((2,)),
        dma((12,)), dma((136,)), dma((2, 4)), dma((16,)), dma((16,)), dma((MP,)), dma((8,)), dma((8,)), dma((8,)),
        dma((2 * F,)), dma((8,)), dma((2 * F,)),
    ]
    sds = jax.ShapeDtypeStruct
    blend, g, both = pl.pallas_call(
        main_kernel,
        out_shape=(sds((MP, 3, COLS), f32), sds((8, 2, PAY), f32), sds((2 * F, 1, D), f32)),
        in_specs=[any_spec] * 9,
        out_specs=(any_spec,) * 3,
        scratch_shapes=scratch,
        compiler_params=pltpu.CompilerParams(
            collective_id=0, has_side_effects=True, vmem_limit_bytes=56 * 1024 * 1024
        ),
        name="tile_gradients",
    )(latent, reward_grad, curvature, counts, w_in, w_value, w_gate, w_down, w_out.T)
    *outs, grad_out = pl.pallas_call(
        final_kernel,
        out_shape=(
            sds((SLAB, COLS), f32), sds((F, D), f32), sds((D, D), f32), sds((D, D), f32), sds((D, D), f32),
            sds((F, D), f32),
        ),
        in_specs=[any_spec] * 5,
        out_specs=(any_spec,) * 6,
        scratch_shapes=[
            vm((MP, 3, COLS), f32), vm((8, 2, PAY), f32), vm((2 * F, 1, D), f32), vm((F, D), bf16), vm((F, D), bf16),
            vm((F, PAY), f32), vm((SLAB, COLS), f32), vm((2 * F, D), f32), vm((3, D, D), f32), dma((5,)), dma((9,)),
        ],
        name="weight_outputs",
    )(blend, g, both, w_in, w_out.T)
    return (*outs, grad_out.T)


def solution(mesh):
    return jax.shard_map(
        per_device,
        mesh=mesh,
        in_specs=(
            P("tile", None), P("tile", None), P("tile", None), P("tile", None), P("tile", None), P(),
            P(None, "mp"), P(None, "mp"), P("mp", None), P(),
        ),
        out_specs=(P("tile", None), P(), P(None, "mp"), P(None, "mp"), P("mp", None), P()),
        check_vma=False,
    )
```

```python
import functools
import math

import jax
import jax.numpy as jnp
from jax import lax
from jax.experimental import pallas as pl
from jax.experimental.pallas import tpu as pltpu
from jax.sharding import PartitionSpec as P

MESH = pl.DeviceIdType.MESH
bf16 = jnp.bfloat16
f32 = jnp.float32

SIDE = 32
HALF = 16
SPACING = 24
JITTER = 4
CH = 4
F = 16
D = 640
COLS = 384
CELLS = 96
SLAB = 12
REGION = 48
GRID_ROWS = 32
MP = 4
TILES = 128
layer_eps = 1e-05
root_half = 0.7071067811865476
inv_root_two_pi = 0.3989422804014327
SCALE = 16.0 / math.sqrt(TILES * HALF * HALF)
PAY = 3 * D
LINK = bf16
WIN = 256


def dot(left, right, dims=((1,), (0,))):
    return lax.dot_general(left, right, (dims, ((), ())), preferred_element_type=f32)


NT = ((1,), (1,))
TN = ((0,), (0,))


def iota(shape, dim):
    return lax.broadcasted_iota(jnp.int32, shape, dim)


def one_hot(cond):
    return jnp.where(cond, 1.0, 0.0).astype(bf16)


def split3(x):
    hi = x.astype(bf16)
    rest = x - hi.astype(f32)
    mid = rest.astype(bf16)
    lo = (rest - mid.astype(f32)).astype(bf16)
    return hi, mid, lo


def split2(x):
    hi = x.astype(bf16)
    return hi, (x - hi.astype(f32)).astype(bf16)


def feature_of(lane):
    return (lane // 128) * 8 + lane % 8


def main_kernel(
    lat_h, rew_h, cur_h, cnt_h, win_h, wv_h, wg_h, wd_h, wo_h,
    blend_o, g_o, p_o,
    lat_s, cnt_s, rew_v, cur_v, win_v, wv, wg, wd, wo_v,
    regf, cntf, x_s, hid_s, gel_s, vs_s, q_s, act_s,
    part_s, rs_send, rs_in, cot_in, blend_in, cot_mine, blend_mine, wdo_s, woe_s, wrep_s,
    pay_s, pay_send, pay_in, z_in, z_mine, g_in, ps_s, ps_send, ps_in, pz_in, pz_mine, p_in,
    lat_own, cnt_own, relay_sem, slab_sem, many_sem,
    loc_sem, send_sem, halo_sem, rs_sem, cot_sem, blend_sem, pay_sem, z_sem, g_sem, ps_sem, pz_sem, p_sem,
):
    t = lax.axis_index("tile")
    p = lax.axis_index("mp")
    plane = t // 8
    member = t % 8
    base8 = plane * 8
    chip = t // 2
    k = t % 2
    across = t % 8 // 2
    odd = plane % 2

    def snake(row):
        z, r = row // 4, row % 4
        return 4 * z + jnp.where(z % 2 == 1, 3 - r, r)

    def shifted(row, n):
        return (row + n + GRID_ROWS) % GRID_ROWS

    grid_row = snake(chip)
    mirror = grid_row
    up_chip = snake(shifted(grid_row, -1))
    down_chip = snake(shifted(grid_row, 1))
    near_n = snake(shifted(chip, 2 * k - 1))
    beside = jnp.where(k == 0, up_chip, down_chip)
    in_place = odd == 0
    far_home = near_n == chip

    loads = []
    for n, (src, dst) in enumerate([
        (lat_h, lat_own), (cnt_h, cnt_own), (wd_h, wd), (wo_h, wo_v), (win_h, win_v), (wv_h, wv), (wg_h, wg),
    ]):
        copy = pltpu.make_async_copy(src, dst, loc_sem.at[n])
        copy.start()
        loads.append(copy)
    slab_loads = [pltpu.make_async_copy(rew_h, rew_v, loc_sem.at[7]), pltpu.make_async_copy(cur_h, cur_v, loc_sem.at[8])]

    @pl.when(in_place)
    def _():
        for copy in slab_loads:
            copy.start()

    own_chip = [((2 * chip + (k + dk) % 2), (p + dq) % MP, (k + dk) % 2) for dk in range(2) for dq in range(MP)][1:]
    group = [(base8 + (member + n) % 8, (member + n) % 8) for n in range(1, 8)]
    every = [
        (base8 + (member + n) % 8, (p + dq) % MP, ((member + n) % 8) * MP + (p + dq) % MP)
        for n in range(8) for dq in range(MP)
    ][1:]
    planes = [(((plane + n) % 8) * 8 + member, (plane + n) % 8) for n in range(1, 8)]

    def hello(sem, target):
        pl.semaphore_signal(sem, inc=1, device_id=target, device_id_type=MESH)

    sides = [(t, (p + 1) % MP), (t, (p + MP - 1) % MP)]
    levels = [(planes[0][0], p), (planes[6][0], p)]
    along = [(2 * up_chip + k, p), (2 * down_chip + k, p)]
    barrier = pltpu.get_barrier_semaphore()
    near = [(2 * mirror + 1 - k, p), (2 * near_n + 1 - k, p), (2 * mirror + 1 - k, p)]
    near += [(2 * chip + 1 - k, p)] + sides + levels + along
    near += [(2 * up_chip + 1 - k, p), (2 * down_chip + 1 - k, p)]
    for target in near:
        hello(barrier, target)
    maybe = [
        2 * mirror + k, 2 * near_n + k, 2 * mirror + k,
        2 * shifted(grid_row, -1) + 1, 2 * shifted(grid_row, 1),
    ]
    count = len(near)
    for target in maybe:
        @pl.when(target != t)
        def _():
            hello(barrier, (target, p))

        count = count + jnp.where(target != t, 1, 0)

    loads[0].wait()
    loads[1].wait()
    pl.semaphore_wait(barrier, count)
    sent = []

    def remote(src, dst, n, sem, target):
        return pltpu.make_async_remote_copy(
            src_ref=src, dst_ref=dst, send_sem=send_sem.at[n], recv_sem=sem,
            device_id=target, device_id_type=MESH,
        )

    def send(src, dst, sem, target, group_sem=None):
        if group_sem is None:
            copy = remote(src, dst, len(sent), sem, target)
            sent.append((None, copy))
        else:
            copy = pltpu.make_async_remote_copy(
                src_ref=src, dst_ref=dst, send_sem=many_sem.at[group_sem], recv_sem=sem,
                device_id=target, device_id_type=MESH,
            )
        copy.start()

    def all_sent(ref, group_sem):
        pltpu.make_async_remote_copy(
            src_ref=ref, dst_ref=ref, send_sem=many_sem.at[group_sem], recv_sem=many_sem.at[group_sem],
            device_id=(t, p), device_id_type=MESH,
        ).wait_send()

    def send_if(cond, src, dst, sem, target):
        copy = remote(src, dst, len(sent), sem, target)

        @pl.when(cond)
        def _():
            copy.start()

        sent.append((cond, copy))

    def arrive(dst, sem):
        remote(dst, dst, 0, sem, (t, p)).wait_recv()

    far_slot = 3 * (1 - k)
    for chip_to, slot, home in ((near_n, far_slot, far_home), (mirror, 1 + k, in_place)):
        for n, (own, slots) in enumerate(((lat_own, lat_s), (cnt_own, cnt_s))):
            send(own, slots.at[slot], halo_sem.at[n, slot], (2 * chip_to + 1 - k, p))
            send_if(jnp.logical_not(home), own, slots.at[slot], halo_sem.at[n, slot], (2 * chip_to + k, p))

        @pl.when(home)
        def _():
            lat_s[slot] = lat_own[...]
            cnt_s[slot] = cnt_own[...]

    for n, (src, dst) in enumerate(((rew_h, rew_v), (cur_h, cur_v))):
        send_if(odd == 1, src, dst, slab_sem.at[n], (2 * mirror + k, p))

    def tell(step, targets):
        for target in targets:
            hello(relay_sem.at[step], target)

    def hear(step):
        pl.semaphore_wait(relay_sem.at[step], 2)

    tell(0, sides)
    tell(4, levels)

    lane256 = iota((1, 256), 1)
    expand = one_hot(iota((F, 256), 0) == feature_of(iota((F, 256), 1)))
    tj_mask = (iota((HALF, 1, 256), 2) % 128) // 8 == iota((HALF, 1, 256), 0)

    for copy in loads[2:5]:
        copy.wait()
    woe = dot(wo_v[...], expand, TN).astype(bf16)
    woe_s[...] = woe
    wdo = dot(wd[...], woe)
    wdo_hi, wdo_lo = split2(wdo)
    wdo_s[0] = wdo_hi
    wdo_s[1] = wdo_lo
    win = win_v[...]
    wrep_s[...] = dot(expand, win, TN).astype(bf16)

    def arrive_halo(slot):
        arrive(lat_s.at[slot], halo_sem.at[0, slot])
        arrive(cnt_s.at[slot], halo_sem.at[1, slot])

    arrive_halo(2 - k)
    for slot, remote_slot in (
        (1 + k, odd == 1),
        (0, 2 * shifted(grid_row, -1) + 1 != t),
        (3, 2 * shifted(grid_row, 1) != t),
    ):
        @pl.when(remote_slot)
        def _():
            arrive_halo(slot)

    hear(0)
    hear(4)
    tell(1, sides)
    tell(5, levels)

    for slot in range(4):
        slab = lat_s[slot].astype(f32)
        regf[SLAB * slot : SLAB * slot + SLAB, :] = jnp.where(k == 0, slab[:, 0:WIN], slab[:, COLS - WIN : COLS])
        cntf[SLAB * slot : SLAB * slot + SLAB, :] = cnt_s[slot].astype(f32)

    lane96 = iota((8, CELLS), 1)
    row_win = jnp.where(cntf[8:16, :] == 2.0, 1.0, 0.0)
    col_win = jnp.where(cntf[24:32, :] == 2.0, 1.0, 0.0)
    first_row = iota((8, CELLS), 0) == 0
    selects = []
    for j in range(2):
        c = 2 * k + j
        n_row = jnp.sum(jnp.where(lane96 == SPACING * c + 12, row_win, 0.0), axis=1, keepdims=True)
        n_row = jnp.sum(n_row, axis=0, keepdims=True)
        row = 16.0 - n_row
        row = jnp.where(grid_row == 0, 12.0, jnp.where(grid_row == GRID_ROWS - 1, 4.0, row))
        near = first_row & (lane96 >= SPACING * c - JITTER) & (lane96 < SPACING * c + JITTER)
        n_col = jnp.sum(jnp.where(near, col_win, 0.0), axis=1, keepdims=True)
        n_col = jnp.sum(n_col, axis=0, keepdims=True)
        col = (SPACING * c + JITTER).astype(f32) - n_col
        col = jnp.where(c == 0, 0.0, jnp.where(c == 3, float(CELLS - SIDE), col))
        m = iota((SIDE, REGION), 0)
        pick = (2 * (m % HALF) + m // HALF).astype(f32) + row
        sel_r = one_hot(iota((SIDE, REGION), 1).astype(f32) == pick)
        shift = CH * col - ((COLS - WIN) * k).astype(f32)
        sel_c = one_hot(iota((WIN, 128), 0).astype(f32) == iota((WIN, 128), 1).astype(f32) + shift)
        m = iota((REGION, 3 * SIDE), 1) % SIDE
        pick = (2 * (m % HALF) + m // HALF).astype(f32) + row
        put_r = one_hot(iota((REGION, 3 * SIDE), 0).astype(f32) == pick)
        selects.append((sel_r, sel_c, put_r))

    def patches_of(region):
        tiles = []
        for sel_r, sel_c, _ in selects:
            rows = dot(sel_r, region).astype(bf16)
            crop = dot(rows, sel_c)
            pair = jnp.concatenate([crop[:HALF], crop[HALF:]], axis=1)
            full = jnp.where(tj_mask, pair.reshape(1, HALF, 256), 0.0)
            tiles.append(full.reshape(HALF * HALF, 256))
        return jnp.concatenate(tiles, axis=0)

    xf = patches_of(regf[...].astype(bf16))
    x = xf.astype(bf16)
    x_s[...] = x
    hidden = dot(x, wrep_s[...]).astype(bf16)
    hid_s[...] = hidden
    values = hidden.astype(f32)
    center = values - jnp.mean(values, axis=-1, keepdims=True)
    variance = jnp.mean(center * center, axis=-1, keepdims=True)
    inv = lax.rsqrt(variance + layer_eps)
    unit = (center * inv).astype(bf16)

    loads[5].wait()
    loads[6].wait()
    value = dot(unit, wv[...])
    gate = dot(unit, wg[...])
    phi = 0.5 * (1.0 + lax.erf(gate * root_half))
    gel = gate * phi
    act = (value * gel).astype(bf16)
    act_s[...] = act
    gel_s[...] = gel
    slope = value * (phi + gate * jnp.exp(-0.5 * gate * gate) * inv_root_two_pi)
    vs_s[...] = slope
    q_s[...] = gel * value + slope * gate

    noise = dot(act, wdo_s[0]) + dot(act, wdo_s[1])
    own = dot(hid_s[...], woe_s[...])
    noise = noise + jnp.where(p == 0, own, 0.0)
    placed = None
    for j in range(2):
        block = noise[256 * j : 256 * j + 256].reshape(HALF, HALF, 256)
        crop = jnp.sum(jnp.where(tj_mask, block, 0.0), axis=0)
        stack = jnp.concatenate(
            [part[:, 128 * a : 128 * a + 128] for part in split3(crop) for a in range(2)], axis=0
        )
        wide = dot(stack, selects[j][1], NT).astype(bf16)
        term = dot(selects[j][2], wide)
        placed = term if placed is None else placed + term
    part_s[...] = placed
    for g in range(16):
        rs_send[g] = part_s[3 * g : 3 * g + 3, :]

    hear(1)
    hear(5)
    for dev, q, kk in own_chip:
        send(rs_send.at[4 + 4 * kk + q], rs_in.at[4 * k + p], rs_sem.at[0], (dev, q), 0)
    for q in range(MP):
        send(rs_send.at[q], rs_in.at[8 + 4 * k + p], rs_sem.at[0], (2 * up_chip + 1, q), 0)
        send(rs_send.at[12 + q], rs_in.at[8 + 4 * k + p], rs_sem.at[0], (2 * down_chip, q), 0)
    rs_in[4 * k + p] = rs_send[4 + 4 * k + p]

    tell(2, along)
    tell(6, levels)

    xi = xf * inv
    xi_hi, xi_lo = split2(xi)
    pt = dot(expand, x, NT).astype(bf16)
    pit = jnp.concatenate([dot(expand, xi_hi, NT).astype(bf16), dot(expand, xi_lo, NT).astype(bf16)], axis=0)

    @pl.when(in_place)
    def _():
        for copy in slab_loads:
            copy.wait()

    @pl.when(odd == 1)
    def _():
        arrive(rew_v, slab_sem.at[0])
        arrive(cur_v, slab_sem.at[1])

    spread = one_hot(iota((CELLS, COLS), 0) == iota((CELLS, COLS), 1) // CH)
    cover = dot(cnt_s[1 + k].astype(f32).astype(bf16), spread)
    rew = rew_v[...]
    cur = cur_v[...]

    def my_rows(slab):
        out = slab[0:3]
        for q in range(1, MP):
            out = jnp.where(p == q, slab[3 * q : 3 * q + 3], out)
        return out

    cover3 = my_rows(cover)
    rew3 = my_rows(rew)
    cur3 = my_rows(cur)

    arrive(rs_in.at[0:15], rs_sem.at[0])
    sums = []
    for kk in range(2):
        part = rs_in[4 * kk]
        for slot in [4 * kk + 1, 4 * kk + 2, 4 * kk + 3] + [8 + 4 * kk + q for q in range(MP)]:
            part = part + rs_in[slot]
        sums.append(part)
    left, right = sums
    total = jnp.concatenate([left[:, 0:128], left[:, 128:] + right[:, 0:128], right[:, 128:]], axis=1)
    blend3 = total / cover3
    cot3 = ((rew3 - cur3 * blend3) / cover3 * SCALE).astype(bf16).astype(f32)
    blend_mine[...] = blend3
    cot_mine[0] = cot3[:, 0:WIN]
    cot_mine[1] = cot3[:, COLS - WIN : COLS]
    for dev, q, kk in own_chip:
        send(cot_mine.at[kk], cot_in.at[4 + 4 * k + p], cot_sem.at[0], (dev, q), 1)
    slot = 12 * (1 - k) + p
    for kk in range(2):
        for q in range(MP):
            send(cot_mine.at[kk], cot_in.at[slot], cot_sem.at[0], (2 * beside + kk, q), 1)
    hear(2)
    hear(6)
    tell(3, along)
    cot_in[4 + 4 * k + p] = cot_mine[k]

    arrive(cot_in.at[0:15], cot_sem.at[0])
    hear(3)
    for dq in range(1, MP):
        send(blend_mine, blend_in.at[p], blend_sem.at[p], (2 * mirror + k, (p + dq) % MP))
    send_if(odd == 1, blend_mine, blend_in.at[p], blend_sem.at[p], (2 * mirror + k, p))

    @pl.when(in_place)
    def _():
        blend_in[p] = blend_mine[...]

    for g in range(16):
        regf[3 * g : 3 * g + 3, :] = cot_in[g]

    y = patches_of(regf[...].astype(bf16)).astype(bf16)
    dfb = dot(y, woe_s[...], NT).astype(bf16)
    d_act = dot(dfb, wd[...], NT)
    dv = (d_act * gel_s[...]).astype(bf16)
    dg = (d_act * vs_s[...]).astype(bf16)
    ct = dot(expand, y, NT).astype(bf16)
    gv = dot(pit, dv)
    gg = dot(pit, dg)
    gv = gv[:F] + gv[F:]
    gg = gg[:F] + gg[F:]
    gd = dot(ct, act_s[...])
    pay_s[:, 0:D] = gv
    pay_s[:, D : 2 * D] = gg
    pay_s[:, 2 * D : 3 * D] = gd
    for c in range(8):
        pay_send[c] = pay_s[2 * c : 2 * c + 2, :].astype(pay_send.dtype)

    for dev, c in group:
        send(pay_send.at[c], pay_in.at[member], pay_sem.at[0], (dev, p), 2)
    pay_in[member] = pay_send[member]

    def rows_dot(piece, right, dims=((1,), (0,))):
        both = dot(jnp.concatenate(split2(piece), axis=0), right, dims)
        return both[:F] + both[F:]

    m2 = jnp.sum(d_act * q_s[...], axis=1, keepdims=True) * (1.0 / D)
    xm_hi, xm_lo = split2(xi * m2)
    b_w = dot(pit, xm_hi) + dot(pit, xm_lo)
    b_w = b_w[:F] + b_w[F:]
    inner = rows_dot(gv, wv[...], NT) + rows_dot(gg, wg[...], NT) - rows_dot(b_w, wrep_s[...])
    inner = inner - jnp.mean(inner, axis=1, keepdims=True)
    ps_s[0:F, :] = inner + 0.25 * rows_dot(dot(pt, y), woe_s[...], NT)
    ps_s[F : 2 * F, :] = rows_dot(gd, wd[...]) + 0.25 * rows_dot(dot(ct, x_s[...]), wrep_s[...])
    for n in range(2 * F):
        ps_send[n] = ps_s[n : n + 1, :]
    mine = MP * member + p
    for dev, q, n in every:
        send(ps_send.at[n], ps_in.at[mine], ps_sem.at[0], (dev, q), 4)
    ps_in[mine] = ps_send[mine]

    arrive(pay_in.at[0:7], pay_sem.at[0])
    rows = pay_in[0].astype(f32)
    for c in range(1, 8):
        rows = rows + pay_in[c].astype(f32)
    z_mine[...] = rows.astype(z_mine.dtype)
    for dev, c in planes:
        send(z_mine, z_in.at[plane], z_sem.at[0], (dev, p), 3)
    z_in[plane] = z_mine[...]

    arrive(ps_in.at[0 : 2 * F - 1], ps_sem.at[0])
    row = ps_in[0]
    for n in range(1, 2 * F):
        row = row + ps_in[n]
    pz_mine[...] = row
    for dev, c in planes:
        send(pz_mine, pz_in.at[plane], pz_sem.at[0], (dev, p), 5)
    pz_in[plane] = row

    arrive(z_in.at[0:7], z_sem.at[0])
    rows = z_in[0].astype(f32)
    for c in range(1, 8):
        rows = rows + z_in[c].astype(f32)
    g_in[member] = rows
    for dev, c in group:
        send(g_in.at[member], g_in.at[member], g_sem.at[0], (dev, p), 6)

    arrive(pz_in.at[0:7], pz_sem.at[0])
    row = pz_in[0]
    for c in range(1, 8):
        row = row + pz_in[c]
    p_in[mine] = row
    for dev, q, n in every:
        send(p_in.at[mine], p_in.at[mine], p_sem.at[0], (dev, q), 7)

    for dq in range(1, MP):
        q = (p + dq) % MP
        arrive(blend_in.at[q], blend_sem.at[q])

    @pl.when(odd == 1)
    def _():
        arrive(blend_in.at[p], blend_sem.at[p])

    outs = [(blend_in, blend_o), (g_in, g_o), (p_in, p_o)]
    outs = [pltpu.make_async_copy(src, dst, loc_sem.at[9 + n]) for n, (src, dst) in enumerate(outs)]
    outs[0].start()
    arrive(g_in.at[0:7], g_sem.at[0])
    outs[1].start()
    arrive(p_in.at[0 : 2 * F - 1], p_sem.at[0])
    outs[2].start()
    for n, ref in enumerate((
        rs_in.at[0:15], cot_in.at[0:15], pay_in.at[0:7], z_in.at[0:7], ps_in.at[0 : 2 * F - 1], pz_in.at[0:7],
        g_in.at[0:7], p_in.at[0 : 2 * F - 1],
    )):
        all_sent(ref, n)
    for cond, copy in sent:
        if cond is None:
            copy.wait_send()
        else:
            pl.when(cond)(copy.wait_send)
    for copy in outs:
        copy.wait()

def final_kernel(
    blend_h, g_h, both_h, win_h, wo_h, blend_o, gin_o, gv_o, gg_o, gd_o, gout_o,
    blend_v, g_v, both_v, win_v, wo_v, g, blend_s, both_s, out_s, in_sem, out_sem,
):
    loads = [
        pltpu.make_async_copy(src, dst, in_sem.at[n])
        for n, (src, dst) in enumerate(
            ((g_h, g_v), (win_h, win_v), (wo_h, wo_v), (blend_h, blend_v), (both_h, both_v))
        )
    ]
    for copy in loads:
        copy.start()
    for copy in loads[:3]:
        copy.wait()
    for c in range(8):
        g[2 * c : 2 * c + 2, :] = g_v[c]
    w = win_v[...]
    w3 = jnp.concatenate([w, w, w], axis=0)
    mean = jnp.mean(w.astype(f32), axis=1, keepdims=True)
    wot = wo_v[...]
    wot3 = jnp.concatenate([wot, wot, wot], axis=0)
    half = D // 2
    copies = []

    def put(src, dst):
        copy = pltpu.make_async_copy(src, dst, out_sem.at[len(copies)])
        copy.start()
        copies.append(copy)

    for n, out in enumerate((gv_o, gg_o, gd_o)):
        rows = g[:, D * n : D * n + D]
        stack = jnp.concatenate(split3(rows), axis=0)
        left, right = (w3, stack) if n < 2 else (stack, wot3)
        for h in range(2):
            block = dot(left[:, half * h : half * h + half], right, TN)
            if n < 2:
                block = block - jnp.sum(mean * rows, axis=0, keepdims=True)
            out_s[n, half * h : half * h + half, :] = block
            put(out_s.at[n, pl.ds(half * h, half)], out.at[pl.ds(half * h, half)])
    for copy in loads[3:]:
        copy.wait()
    for q in range(MP):
        blend_s[3 * q : 3 * q + 3, :] = blend_v[q]
    for n in range(2 * F):
        both_s[n : n + 1, :] = both_v[n]
    put(blend_s, blend_o)
    put(both_s.at[0:F], gin_o)
    put(both_s.at[F : 2 * F], gout_o)
    for copy in copies:
        copy.wait()


def per_device(latent, reward_grad, curvature, offsets, counts, w_in, w_value, w_gate, w_down, w_out):
    vm = pltpu.VMEM
    any_spec = pl.BlockSpec(memory_space=pl.ANY)
    tokens = 2 * HALF * HALF
    dma = pltpu.SemaphoreType.DMA
    scratch = [
        vm((4, SLAB, COLS), bf16), vm((4, SLAB, CELLS), jnp.int32), vm((SLAB, COLS), f32), vm((SLAB, COLS), f32),
        vm((F, D), bf16), vm((D, D), bf16), vm((D, D), bf16), vm((D, D), bf16), vm((F, D), bf16),
        vm((REGION, WIN), f32), vm((REGION, CELLS), f32), vm((tokens, 256), bf16), vm((tokens, D), bf16),
        vm((tokens, D), f32), vm((tokens, D), f32), vm((tokens, D), f32), vm((tokens, D), bf16),
        vm((REGION, WIN), f32), vm((16, 3, WIN), f32), vm((16, 3, WIN), f32), vm((16, 3, WIN), f32),
        vm((MP, 3, COLS), f32), vm((2, 3, WIN), f32), vm((3, COLS), f32), vm((2, D, 256), bf16), vm((D, 256), bf16),
        vm((256, D), bf16),
        vm((F, PAY), f32), vm((8, 2, PAY), LINK), vm((8, 2, PAY), LINK), vm((8, 2, PAY), LINK), vm((2, PAY), LINK),
        vm((8, 2, PAY), f32), vm((2 * F, D), f32), vm((2 * F, 1, D), f32), vm((2 * F, 1, D), f32), vm((8, 1, D), f32),
        vm((1, D), f32), vm((2 * F, 1, D), f32),
        vm((SLAB, COLS), bf16), vm((SLAB, CELLS), jnp.int32), pltpu.SemaphoreType.REGULAR((7,)), dma((2,)), dma((8,)),
        dma((12,)), dma((16,)), dma((2, 4)), dma((1,)), dma((1,)), dma((MP,)), dma((1,)), dma((1,)), dma((1,)),
        dma((1,)), dma((1,)), dma((1,)),
    ]
    sds = jax.ShapeDtypeStruct
    blend, g, both = pl.pallas_call(
        main_kernel,
        out_shape=(sds((MP, 3, COLS), f32), sds((8, 2, PAY), f32), sds((2 * F, 1, D), f32)),
        in_specs=[any_spec] * 9,
        out_specs=(any_spec,) * 3,
        scratch_shapes=scratch,
        compiler_params=pltpu.CompilerParams(
            collective_id=0, has_side_effects=True, vmem_limit_bytes=56 * 1024 * 1024
        ),
        name="tile_gradients",
    )(latent, reward_grad, curvature, counts, w_in, w_value, w_gate, w_down, w_out.T)
    *outs, grad_out = pl.pallas_call(
        final_kernel,
        out_shape=(
            sds((SLAB, COLS), f32), sds((F, D), f32), sds((D, D), f32), sds((D, D), f32), sds((D, D), f32),
            sds((F, D), f32),
        ),
        in_specs=[any_spec] * 5,
        out_specs=(any_spec,) * 6,
        scratch_shapes=[
            vm((MP, 3, COLS), f32), vm((8, 2, PAY), f32), vm((2 * F, 1, D), f32), vm((F, D), bf16), vm((F, D), bf16),
            vm((F, PAY), f32), vm((SLAB, COLS), f32), vm((2 * F, D), f32), vm((3, D, D), f32), dma((5,)), dma((9,)),
        ],
        name="weight_outputs",
    )(blend, g, both, w_in, w_out.T)
    return (*outs, grad_out.T)


def solution(mesh):
    return jax.shard_map(
        per_device,
        mesh=mesh,
        in_specs=(
            P("tile", None), P("tile", None), P("tile", None), P("tile", None), P("tile", None), P(),
            P(None, "mp"), P(None, "mp"), P("mp", None), P(),
        ),
        out_specs=(P("tile", None), P(), P(None, "mp"), P(None, "mp"), P("mp", None), P()),
        check_vma=False,
    )
```
